128 devices in a mesh: row: 4 (over x_hi, core), col: 32 (over z, y, x_lo).
Axes of the slice: x: 4 (x_hi: 2, x_lo: 2; x = x_hi * 2 + x_lo), y: 4, z: 4, core: 2. Of those that a mesh axis runs over, the one named last changes fastest.
Arguments:
- amplitudes: bfloat16 [2048, 16384], P(('row', 'col')), may hold values from -6 to 6
- integrals: bfloat16 [32768, 16384], P('col', 'row'), may hold values from -0.21875 to 0.21875
- orbital_irrep: int32 [1024], replicated, may hold values from 0 to 7
- orbital_spin: int32 [1024], replicated, may hold values from 0 to 1
Outputs:
- residual_tiles: bfloat16 [2048, 32768], P('row', 'col')
The draws below stay inside these ranges and needn't reach their ends.
All inputs are finite; a program needn't handle non-finite values.
Results may differ from the reference program's by a relative error of at most 0.001.
Values may be sent and summed in bfloat16 or wider, within the bound.
A program may use at most 128 MiB of HBM per device.

```python
import jax
import jax.numpy as jnp
from jax import lax

NVIR = 1024
PAIRS = 2048
A_TOT = 32
C_TOT = 16
AB = 32768
CD = 16384


def touch_ends(entries, rng, least, largest):
    longest = entries.shape.index(max(entries.shape))
    spots = []
    for shift in (0, 1):
        where = [jax.random.randint(jax.random.fold_in(rng, axis), (), 0, length) for axis, length in enumerate(entries.shape)]
        where[longest] = (where[longest] + shift) % entries.shape[longest]
        spots.append(tuple(where))
    return entries.at[spots[0]].set(least).at[spots[1]].set(largest)


def level_of(key, shape, pieces, smallest, high):
    loudness, own = 1.0, jax.random.fold_in(key, 6)
    for axis_at, blocks in pieces:
        heights = jnp.exp(jax.random.uniform(jax.random.fold_in(own, axis_at), (blocks,), jnp.float32, smallest / len(pieces), high / len(pieces)))
        loudness = loudness * jnp.repeat(heights, shape[axis_at] // blocks).reshape([-1 if axis == axis_at else 1 for axis in range(len(shape))])
    return loudness


def scatter_about(key, shape, scale, most, split=(), held_as=jnp.bfloat16):
    drawn = scale * jax.random.normal(key, shape, jnp.float32)
    if split:
        drawn = drawn * level_of(key, shape, split, -0.22, 0.18)
    return jnp.clip(drawn, -most, most).astype(held_as)


def setup_inputs(seed: int = 0) -> dict:
    key_list = jax.random.split(jax.random.key(seed), 5)
    return {
        "amplitudes": scatter_about(key_list[0], (PAIRS, CD), 1.0, 6.0, ((0, 128),)),
        "integrals": scatter_about(key_list[1], (AB, CD), (CD // 20) ** -0.5, 0.21875, ((0, 32), (1, 4))),
        "orbital_irrep": touch_ends(jax.random.randint(key_list[2], (NVIR,), 0, 8), jax.random.fold_in(key_list[2], 1), 0, 7).astype(jnp.int32),
        "orbital_spin": touch_ends(jax.random.randint(key_list[3], (NVIR,), 0, 2), jax.random.fold_in(key_list[3], 1), 0, 1).astype(jnp.int32),
    }


def reference(amplitudes, integrals, orbital_irrep, orbital_spin):
    c_index = jnp.arange(C_TOT, dtype=jnp.int32)
    cd_labels = (jnp.bitwise_xor(orbital_irrep[c_index][:, None], orbital_irrep[None, :])
                 + 8 * (orbital_spin[c_index][:, None] + orbital_spin[None, :])).reshape(-1)
    table = amplitudes.astype(jnp.float32)

    def one_block(index):
        rows = lax.dynamic_slice_in_dim(integrals, (index * NVIR).astype(jnp.int32), NVIR, 0)
        ab_labels = jnp.bitwise_xor(orbital_irrep[index], orbital_irrep) + 8 * (orbital_spin[index] + orbital_spin)
        masked = jnp.where(ab_labels[:, None] == cd_labels[None, :], rows, jnp.zeros((), rows.dtype))
        return jnp.dot(table, masked.astype(jnp.float32).T, precision=lax.Precision.HIGHEST)

    blocks = lax.map(one_block, jnp.arange(A_TOT, dtype=jnp.int32))
    return blocks.transpose(1, 0, 2).reshape(PAIRS, A_TOT * NVIR).astype(jnp.bfloat16)
```

```python
import functools

import jax
import jax.numpy as jnp
from jax import lax
from jax.experimental import pallas as pl
from jax.experimental.pallas import tpu as pltpu
from jax.sharding import PartitionSpec as P

MESH = pl.DeviceIdType.MESH
CLASSES = 16
SLOTS = 96
RING = 4
PER_Z = CLASSES // RING
LANES = 128
MIB = 1 << 20


def nt_dot(lhs, rhs):
    return lax.dot_general(lhs, rhs, (((1,), (1,)), ((), ())), preferred_element_type=jnp.float32)


def nn_dot(lhs, rhs):
    return jnp.dot(lhs, rhs, preferred_element_type=jnp.float32)


def pair_labels(first, count, orbital_irrep, orbital_spin):
    lead_irrep = lax.dynamic_slice_in_dim(orbital_irrep, first, count, 0)
    lead_spin = lax.dynamic_slice_in_dim(orbital_spin, first, count, 0)
    labels = jnp.bitwise_xor(lead_irrep[:, None], orbital_irrep[None, :]) + 8 * (
        lead_spin[:, None] + orbital_spin[None, :]
    )
    return labels.reshape(-1)


def dense(amplitudes, integrals, orbital_irrep, orbital_spin):
    virtuals = orbital_irrep.shape[0]
    a_count = integrals.shape[0] // virtuals
    c_count = integrals.shape[1] // virtuals
    ab_labels = pair_labels(lax.axis_index("col") * a_count, a_count, orbital_irrep, orbital_spin)
    cd_labels = pair_labels(lax.axis_index("row") * c_count, c_count, orbital_irrep, orbital_spin)
    masked = jnp.where(
        ab_labels[:, None] == cd_labels[None, :], integrals, jnp.zeros((), integrals.dtype)
    )
    grid_rows = lax.all_gather(amplitudes, "col", axis=0, tiled=True)
    regrouped = lax.all_to_all(grid_rows, "row", split_axis=1, concat_axis=0, tiled=True)
    partial_sums = nt_dot(regrouped, masked)
    return lax.psum_scatter(partial_sums, "row", scatter_dimension=0, tiled=True).astype(
        jnp.bfloat16
    )


def pack_quad(pieces):
    first, second, third, fourth = pieces
    lane = lax.broadcasted_iota(jnp.int32, first.shape, 1)
    zero = jnp.zeros_like(first)
    second = pltpu.roll(second, 96, 1)
    third = pltpu.roll(third, 64, 1)
    fourth = pltpu.roll(fourth, 32, 1)
    return (
        first + jnp.where(lane >= 96, second, zero),
        jnp.where(lane < 64, second, zero) + jnp.where(lane >= 64, third, zero),
        jnp.where(lane < 32, third, zero) + fourth,
    )


def sort_amplitudes(class_ref, spot_ref, t_ref, out_ref, stacked, sorted_ref):
    pairs, c_tot = t_ref.shape[0], t_ref.shape[1] // spot_ref.shape[0]
    nvir = spot_ref.shape[0]
    for c in range(c_tot):
        stacked[pl.ds(c * pairs, pairs), :] = t_ref[:, pl.ds(c * nvir, nvir)]
    spot = spot_ref[...]
    for pair in range(CLASSES // 2):
        column = lax.broadcasted_iota(jnp.int32, (nvir, 2 * LANES), 1) + pair * 2 * LANES
        pick = jnp.where(spot == column, 1.0, 0.0).astype(jnp.bfloat16)
        got = nn_dot(stacked[...], pick)
        sorted_ref[2 * pair] = got[:, :LANES]
        sorted_ref[2 * pair + 1] = got[:, LANES:]
    for quad in range(c_tot // 4):

        @pl.loop(0, CLASSES)
        def _(h):
            pieces = [
                sorted_ref[jnp.bitwise_xor(h, class_ref[4 * quad + q]), pl.ds((4 * quad + q) * pairs, pairs), :]
                for q in range(4)
            ]
            for part, value in enumerate(pack_quad(pieces)):
                out_ref[h, :, pl.ds(quad * 384 + part * LANES, LANES)] = value.astype(jnp.bfloat16)


def compress_integrals(ab_ref, cd_ref, rank_ref, spot_ref, v_ref, out_ref, picked, packed):
    step = pl.program_id(0)
    rows, nvir = v_ref.shape[0], rank_ref.shape[0]

    @pl.when(step == 0)
    def _():
        lane = lax.broadcasted_iota(jnp.int32, (nvir, LANES), 1)
        picked[...] = jnp.where(rank_ref[...] == lane, 1.0, 0.0).astype(jnp.bfloat16)

    pieces = []
    for c in range(4):
        keep = ab_ref[...] == cd_ref[:, pl.ds(c * nvir, nvir)]
        block = v_ref[:, pl.ds(c * nvir, nvir)]
        masked = jnp.where(keep, block, jnp.zeros_like(block))
        pieces.append(nn_dot(masked, picked[...]))
    for part, value in enumerate(pack_quad(pieces)):
        packed[pl.ds(step * rows, rows), pl.ds(part * LANES, LANES)] = value.astype(jnp.bfloat16)

    @pl.when(step == pl.num_programs(0) - 1)
    def _():
        for z in range(RING):
            size = PER_Z * SLOTS
            row = lax.broadcasted_iota(jnp.int32, (size, nvir), 0) + z * size
            pick = jnp.where(spot_ref[...] == row, 1.0, 0.0).astype(jnp.bfloat16)
            got = nn_dot(pick, packed[...]).astype(jnp.bfloat16)
            for j in range(PER_Z):
                out_ref[z * PER_Z + j] = got[j * SLOTS : (j + 1) * SLOTS]


def contract(
    spot_ref, t_ref, v_ref, out_ref, t_all, v_all, r_mine, r_all, t1s, t1r, v1s, v1r, v2s, v2r, t2s, t2r, rs, rr
):
    row, col = lax.axis_index("row"), lax.axis_index("col")
    z, y, xl = col // 8, (col // 2) % 4, col % 2
    pairs, depth = t_ref.shape[1], t_ref.shape[2]
    block = 8 * pairs
    width = depth // 4
    tall = RING * SLOTS

    def place(z_, y_, xl_):
        return z_ * 8 + y_ * 2 + xl_

    def ring(value, shift):
        return lax.rem(value + (shift + RING), RING)

    core_row = jnp.bitwise_xor(row, 1)
    far_row = ring(row, 2)

    def remote(src, dst, send, recv, row_, col_):
        return pltpu.make_async_remote_copy(
            src_ref=src, dst_ref=dst, send_sem=send, recv_sem=recv, device_id=(row_, col_), device_id_type=MESH
        )

    def t1(j, dz, dx, sending):
        to_z, to_x = ring(z, dz), jnp.bitwise_xor(xl, dx)
        from_z = z if sending else ring(z, -dz)
        from_x = xl if sending else to_x
        here = pl.multiple_of((from_z * 2 + from_x) * pairs, pairs)
        src = t_ref.at[to_z * PER_Z + j]
        dst = t_all.at[0, j, pl.ds(here, pairs), :]
        if dz == 0 and dx == 0:
            return pltpu.make_async_copy(src, dst, t1r.at[j, 0])
        n = dz * 2 + dx
        return remote(src, dst, t1s.at[j, n], t1r.at[j, n], row, place(to_z, y, to_x))

    def v1(j, dz, sending):
        to_z = ring(z, dz)
        from_z = z if sending else ring(z, -dz)
        src = v_ref.at[to_z * PER_Z + j]
        dst = v_all.at[
            j, pl.ds(pl.multiple_of(from_z * SLOTS, SLOTS), SLOTS), pl.ds(pl.multiple_of(row * width, width), width)
        ]
        if dz == 0:
            return pltpu.make_async_copy(src, dst, v1r.at[j, 0])
        return remote(src, dst, v1s.at[j, dz], v1r.at[j, dz], row, place(to_z, y, xl))

    def v2(j, kind, sending):
        if kind == 0:
            of = row if sending else core_row
        elif kind == 1:
            of = row if sending else far_row
        else:
            of = far_row if sending else ring(core_row, 2)
        part = v_all.at[j, :, pl.ds(pl.multiple_of(of * width, width), width)]
        return remote(part, part, v2s.at[j, kind], v2r.at[j, kind], far_row if kind == 1 else core_row, col)

    def t2(j, kind):
        half = block // 2
        up, down = place(z, ring(y, 1), xl), place(z, ring(y, -1), xl)
        if kind == 0:
            src, dst, to = t_all.at[0, j], t_all.at[1, j], up
        elif kind == 1:
            src, dst, to = t_all.at[0, j], t_all.at[2, j], down
        elif kind == 2:
            src, dst, to = t_all.at[1, j, pl.ds(0, half), :], t_all.at[3, j, pl.ds(0, half), :], up
        else:
            src, dst, to = t_all.at[2, j, pl.ds(half, half), :], t_all.at[3, j, pl.ds(half, half), :], down
        return remote(src, dst, t2s.at[j, kind], t2r.at[j, kind], row, to)

    def back(j, s, dz, sending):
        to_z = ring(z, dz)
        from_z = z if sending else ring(z, -dz)
        y_of = ring(y, (0, -1, 1, 2)[s])
        src = r_mine.at[s, j, pl.ds(pl.multiple_of(to_z * SLOTS, SLOTS), SLOTS), :]
        dst = r_all.at[
            pl.ds(pl.multiple_of((from_z * PER_Z + j) * SLOTS, SLOTS), SLOTS),
            pl.ds(pl.multiple_of(y_of * block, block), block),
        ]
        n = s * RING + dz
        if dz == 0:
            return pltpu.make_async_copy(src, dst, rr.at[j, n])
        return remote(src, dst, rs.at[j, n], rr.at[j, n], row, place(to_z, y, xl))

    pushes = [(dz, dx) for dz in (1, 3, 2, 0) for dx in (0, 1)]

    barrier = pltpu.get_barrier_semaphore()
    peers = [(row, place(ring(z, dz), y, jnp.bitwise_xor(xl, dx))) for dz, dx in pushes if dz or dx]
    peers += [(row, place(z, ring(y, 1), xl)), (row, place(z, ring(y, -1), xl)), (core_row, col), (far_row, col)]
    for peer in peers:
        pl.semaphore_signal(barrier, inc=1, device_id=peer, device_id_type=MESH)
    pl.semaphore_wait(barrier, len(peers))

    for j in range(PER_Z):
        for dz, dx in pushes:
            t1(j, dz, dx, True).start()
        for dz in (1, 3, 2, 0):
            v1(j, dz, True).start()

    def arrived(copy):
        if hasattr(copy, "wait_recv") and getattr(copy, "is_remote", True):
            copy.wait_recv()
        else:
            copy.wait()

    def multiply(j, s):
        r_mine[s, j] = nt_dot(v_all[j], t_all[s, j]).astype(jnp.bfloat16)
        for dz in (1, 3, 2, 0):
            back(j, s, dz, True).start()

    for step in range(PER_Z + 3):
        j = step
        if j < PER_Z:
            for dz, dx in pushes:
                arrived(t1(j, dz, dx, False))
            t2(j, 0).start()
            t2(j, 1).start()
            for dz in (1, 3, 2, 0):
                arrived(v1(j, dz, False))
            v2(j, 0, True).start()
            v2(j, 1, True).start()
        j = step - 1
        if 0 <= j < PER_Z:
            arrived(t2(j, 0))
            t2(j, 2).start()
            arrived(t2(j, 1))
            t2(j, 3).start()
            arrived(v2(j, 1, False))
            v2(j, 2, True).start()
        j = step - 2
        if 0 <= j < PER_Z:
            arrived(v2(j, 0, False))
            arrived(v2(j, 2, False))
            for s in range(3):
                multiply(j, s)
        j = step - 3
        if 0 <= j < PER_Z:
            arrived(t2(j, 2))
            arrived(t2(j, 3))
            multiply(j, 3)

    for j in range(PER_Z):
        for s in range(4):
            for dz in range(RING):
                arrived(back(j, s, dz, False))

    nvir = spot_ref.shape[0]
    piece = 256
    for n in range(nvir // piece):
        column = lax.broadcasted_iota(jnp.int32, (piece, CLASSES * SLOTS), 1)
        pick = jnp.where(spot_ref[pl.ds(n * piece, piece), :] == column, 1.0, 0.0).astype(jnp.bfloat16)
        out_ref[pl.ds(n * piece, piece), :] = nn_dot(pick, r_all[...]).astype(jnp.bfloat16)

    for j in range(PER_Z):
        for dz, dx in pushes:
            if dz or dx:
                t1(j, dz, dx, True).wait_send()
        for dz in (1, 3, 2):
            v1(j, dz, True).wait_send()
        for kind in range(3):
            v2(j, kind, True).wait_send()
        for kind in range(4):
            t2(j, kind).wait_send()
        for s in range(4):
            for dz in (1, 3, 2):
                back(j, s, dz, True).wait_send()


def blocked(rank, amplitudes, integrals, orbital_irrep, orbital_spin):
    nvir = orbital_irrep.shape[0]
    pairs, cd = amplitudes.shape
    ab, cd_here = integrals.shape
    c_tot = cd // nvir
    row, col = lax.axis_index("row"), lax.axis_index("col")
    group = orbital_irrep + 8 * orbital_spin
    spot_t = (group * LANES + rank)[:, None]
    own = lax.dynamic_slice_in_dim(group, col, 1, 0)
    spot_b = jnp.bitwise_xor(group, own) * SLOTS + rank
    ab_labels = pair_labels(col, 1, orbital_irrep, orbital_spin)[:, None]
    cd_labels = pair_labels(row * (cd_here // nvir), cd_here // nvir, orbital_irrep, orbital_spin)[None, :]

    vmem = pl.BlockSpec(memory_space=pltpu.VMEM)
    depth = c_tot * SLOTS
    sorted_t = pl.pallas_call(
        sort_amplitudes,
        out_shape=jax.ShapeDtypeStruct((CLASSES, pairs, depth), jnp.bfloat16),
        in_specs=[pl.BlockSpec(memory_space=pltpu.SMEM), vmem, vmem],
        out_specs=vmem,
        scratch_shapes=[
            pltpu.VMEM((c_tot * pairs, nvir), jnp.bfloat16),
            pltpu.VMEM((CLASSES, c_tot * pairs, LANES), jnp.float32),
        ],
        compiler_params=pltpu.CompilerParams(vmem_limit_bytes=40 * MIB),
        name="sort_amplitudes",
    )(group[:c_tot], spot_t, amplitudes)

    rows = 128
    width = (cd_here // nvir) * SLOTS
    packed_v = pl.pallas_call(
        compress_integrals,
        out_shape=jax.ShapeDtypeStruct((CLASSES, SLOTS, width), jnp.bfloat16),
        grid=(ab // rows,),
        in_specs=[
            pl.BlockSpec((rows, 1), lambda i: (i, 0)),
            pl.BlockSpec((1, cd_here), lambda i: (0, 0)),
            pl.BlockSpec((nvir, 1), lambda i: (0, 0)),
            pl.BlockSpec((1, nvir), lambda i: (0, 0)),
            pl.BlockSpec((rows, cd_here), lambda i: (i, 0)),
        ],
        out_specs=pl.BlockSpec((CLASSES, SLOTS, width), lambda i: (0, 0, 0)),
        scratch_shapes=[pltpu.VMEM((nvir, LANES), jnp.bfloat16), pltpu.VMEM((ab, width), jnp.bfloat16)],
        compiler_params=pltpu.CompilerParams(vmem_limit_bytes=40 * MIB),
        name="compress_integrals",
    )(ab_labels, cd_labels, rank[:, None], spot_b[None, :], integrals)

    block = 8 * pairs
    tall = RING * SLOTS
    dma = pltpu.SemaphoreType.DMA
    flipped = pl.pallas_call(
        contract,
        out_shape=jax.ShapeDtypeStruct((nvir, RING * block), jnp.bfloat16),
        in_specs=[vmem] * 3,
        out_specs=vmem,
        scratch_shapes=[
            pltpu.VMEM((RING, PER_Z, block, depth), jnp.bfloat16),
            pltpu.VMEM((PER_Z, tall, depth), jnp.bfloat16),
            pltpu.VMEM((RING, PER_Z, tall, block), jnp.bfloat16),
            pltpu.VMEM((CLASSES * SLOTS, RING * block), jnp.bfloat16),
            dma((PER_Z, 8)),
            dma((PER_Z, 8)),
            dma((PER_Z, 4)),
            dma((PER_Z, 4)),
            dma((PER_Z, 3)),
            dma((PER_Z, 3)),
            dma((PER_Z, 4)),
            dma((PER_Z, 4)),
            dma((PER_Z, 16)),
            dma((PER_Z, 16)),
        ],
        compiler_params=pltpu.CompilerParams(
            collective_id=0, has_side_effects=True, vmem_limit_bytes=48 * MIB
        ),
        name="contract",
    )(spot_b[:, None], sorted_t, packed_v)
    spread = flipped.reshape(nvir, RING, RING, 2 * pairs)
    return spread.transpose(2, 1, 3, 0).reshape(RING * block, nvir)


def local(amplitudes, integrals, orbital_irrep, orbital_spin):
    group = orbital_irrep + 8 * orbital_spin
    count = jnp.arange(group.shape[0], dtype=jnp.int32)
    earlier = (group[:, None] == group[None, :]) & (count[None, :] < count[:, None])
    rank = jnp.sum(earlier.astype(jnp.int32), axis=1)
    return lax.cond(
        jnp.max(rank) < SLOTS,
        blocked,
        lambda rank, *args: dense(*args),
        rank,
        amplitudes,
        integrals,
        orbital_irrep,
        orbital_spin,
    )


def solution(mesh):
    placed = (P(("row", "col"), None), P("col", "row"), P(), P())
    return jax.shard_map(
        local, mesh=mesh, in_specs=placed, out_specs=P("row", "col"), check_vma=False
    )
```

```python
import functools

import jax
import jax.numpy as jnp
from jax import lax
from jax.experimental import pallas as pl
from jax.experimental.pallas import tpu as pltpu
from jax.sharding import PartitionSpec as P

MESH = pl.DeviceIdType.MESH
CLASSES = 16
SLOTS = 96
RING = 4
PER_Z = CLASSES // RING
LANES = 128
MIB = 1 << 20


def nt_dot(lhs, rhs):
    return lax.dot_general(lhs, rhs, (((1,), (1,)), ((), ())), preferred_element_type=jnp.float32)


def nn_dot(lhs, rhs):
    return jnp.dot(lhs, rhs, preferred_element_type=jnp.float32)


def pair_labels(first, count, orbital_irrep, orbital_spin):
    lead_irrep = lax.dynamic_slice_in_dim(orbital_irrep, first, count, 0)
    lead_spin = lax.dynamic_slice_in_dim(orbital_spin, first, count, 0)
    labels = jnp.bitwise_xor(lead_irrep[:, None], orbital_irrep[None, :]) + 8 * (
        lead_spin[:, None] + orbital_spin[None, :]
    )
    return labels.reshape(-1)


def dense(amplitudes, integrals, orbital_irrep, orbital_spin):
    virtuals = orbital_irrep.shape[0]
    a_count = integrals.shape[0] // virtuals
    c_count = integrals.shape[1] // virtuals
    ab_labels = pair_labels(lax.axis_index("col") * a_count, a_count, orbital_irrep, orbital_spin)
    cd_labels = pair_labels(lax.axis_index("row") * c_count, c_count, orbital_irrep, orbital_spin)
    masked = jnp.where(
        ab_labels[:, None] == cd_labels[None, :], integrals, jnp.zeros((), integrals.dtype)
    )
    grid_rows = lax.all_gather(amplitudes, "col", axis=0, tiled=True)
    regrouped = lax.all_to_all(grid_rows, "row", split_axis=1, concat_axis=0, tiled=True)
    partial_sums = nt_dot(regrouped, masked)
    return lax.psum_scatter(partial_sums, "row", scatter_dimension=0, tiled=True).astype(
        jnp.bfloat16
    )


def one_hot(hit):
    return jnp.where(hit, 1.0, 0.0).astype(jnp.bfloat16)


def pack_quad(pieces):
    first, second, third, fourth = pieces
    lane = lax.broadcasted_iota(jnp.int32, first.shape, 1)
    zero = jnp.zeros_like(first)
    second = pltpu.roll(second, 96, 1)
    third = pltpu.roll(third, 64, 1)
    fourth = pltpu.roll(fourth, 32, 1)
    return (
        first + jnp.where(lane >= 96, second, zero),
        jnp.where(lane < 64, second, zero) + jnp.where(lane >= 64, third, zero),
        jnp.where(lane < 32, third, zero) + fourth,
    )


def contract(
    code_s, code_col, code_row, t_ref, v_hbm, out_ref,
    v_raw, stacked, by_class, t_mine, picked, packed, v_mine, unsort, t_all, v_all, r_mine, r_all,
    loads, t1s, t1r, v1s, v1r, v2s, v2r, t2s, t2r, rs, rr,
):
    row, col = lax.axis_index("row"), lax.axis_index("col")
    z, y, xl = col // 8, (col // 2) % 4, col % 2
    nvir = code_col.shape[0]
    pairs, c_tot = t_ref.shape[0], t_ref.shape[1] // nvir
    c_here = v_hbm.shape[1] // nvir
    block = 8 * pairs
    width = c_here * SLOTS
    chunks, rows = v_raw.shape[0], v_raw.shape[1]

    def load(n):
        return pltpu.make_async_copy(v_hbm.at[pl.ds(n * rows, rows), :], v_raw.at[n], loads.at[n])

    for n in range(chunks):
        load(n).start()

    def place(z_, y_, xl_):
        return z_ * 8 + y_ * 2 + xl_

    def ring(value, shift):
        return lax.rem(value + (shift + RING), RING)

    core_row = jnp.bitwise_xor(row, 1)
    far_row = ring(row, 2)

    def remote(src, dst, send, recv, row_, col_):
        return pltpu.make_async_remote_copy(
            src_ref=src, dst_ref=dst, send_sem=send, recv_sem=recv, device_id=(row_, col_), device_id_type=MESH
        )

    def t1(j, dz, dx, sending):
        to_z, to_x = ring(z, dz), jnp.bitwise_xor(xl, dx)
        from_z = z if sending else ring(z, -dz)
        from_x = xl if sending else to_x
        here = pl.multiple_of((from_z * 2 + from_x) * pairs, pairs)
        src = t_mine.at[to_z * PER_Z + j]
        dst = t_all.at[0, j, pl.ds(here, pairs), :]
        if dz == 0 and dx == 0:
            return pltpu.make_async_copy(src, dst, t1r.at[j, 0])
        n = dz * 2 + dx
        return remote(src, dst, t1s.at[j, n], t1r.at[j, n], row, place(to_z, y, to_x))

    def v1(j, dz, sending):
        to_z = ring(z, dz)
        from_z = z if sending else ring(z, -dz)
        src = v_mine.at[to_z * PER_Z + j]
        dst = v_all.at[
            j, pl.ds(pl.multiple_of(from_z * SLOTS, SLOTS), SLOTS), pl.ds(pl.multiple_of(row * width, width), width)
        ]
        if dz == 0:
            return pltpu.make_async_copy(src, dst, v1r.at[j, 0])
        return remote(src, dst, v1s.at[j, dz], v1r.at[j, dz], row, place(to_z, y, xl))

    def v2(j, kind, sending):
        if kind == 0:
            of = row if sending else core_row
        elif kind == 1:
            of = row if sending else far_row
        else:
            of = far_row if sending else ring(core_row, 2)
        part = v_all.at[j, :, pl.ds(pl.multiple_of(of * width, width), width)]
        return remote(part, part, v2s.at[j, kind], v2r.at[j, kind], far_row if kind == 1 else core_row, col)

    def t2(j, kind):
        half = block // 2
        up, down = place(z, ring(y, 1), xl), place(z, ring(y, -1), xl)
        if kind == 0:
            src, dst, to = t_all.at[0, j], t_all.at[1, j], up
        elif kind == 1:
            src, dst, to = t_all.at[0, j], t_all.at[2, j], down
        elif kind == 2:
            src, dst, to = t_all.at[1, j, pl.ds(0, half), :], t_all.at[3, j, pl.ds(0, half), :], up
        else:
            src, dst, to = t_all.at[2, j, pl.ds(half, half), :], t_all.at[3, j, pl.ds(half, half), :], down
        return remote(src, dst, t2s.at[j, kind], t2r.at[j, kind], row, to)

    def back(j, s, dz, sending):
        to_z = ring(z, dz)
        from_z = z if sending else ring(z, -dz)
        y_of = ring(y, (0, -1, 1, 2)[s])
        src = r_mine.at[s, j, pl.ds(pl.multiple_of(to_z * SLOTS, SLOTS), SLOTS), :]
        dst = r_all.at[
            pl.ds(pl.multiple_of((from_z * PER_Z + j) * SLOTS, SLOTS), SLOTS),
            pl.ds(pl.multiple_of(y_of * block, block), block),
        ]
        n = s * RING + dz
        if dz == 0:
            return pltpu.make_async_copy(src, dst, rr.at[j, n])
        return remote(src, dst, rs.at[j, n], rr.at[j, n], row, place(to_z, y, xl))

    pushes = [(dz, dx) for dz in (1, 3, 2, 0) for dx in (0, 1)]

    barrier = pltpu.get_barrier_semaphore()
    peers = [(row, place(ring(z, dz), y, jnp.bitwise_xor(xl, dx))) for dz, dx in pushes if dz or dx]
    peers += [(row, place(z, ring(y, 1), xl)), (row, place(z, ring(y, -1), xl)), (core_row, col), (far_row, col)]
    for peer in peers:
        pl.semaphore_signal(barrier, inc=1, device_id=peer, device_id_type=MESH)

    for c in range(c_tot):
        stacked[pl.ds(c * pairs, pairs), :] = t_ref[:, pl.ds(c * nvir, nvir)]
    for pair in range(CLASSES // 2):
        column = lax.broadcasted_iota(jnp.int32, (nvir, 2 * LANES), 1) + pair * 2 * LANES
        got = nn_dot(stacked[...], one_hot(code_col[...] == column))
        by_class[2 * pair] = got[:, :LANES]
        by_class[2 * pair + 1] = got[:, LANES:]
    classes = [code_s[c] >> 7 for c in range(c_tot)]
    pl.semaphore_wait(barrier, len(peers))
    for j in range(PER_Z):
        for z_ in range(RING):
            h = z_ * PER_Z + j
            for quad in range(c_tot // 4):
                pieces = [
                    by_class[jnp.bitwise_xor(classes[c], h), pl.ds(c * pairs, pairs), :]
                    for c in range(4 * quad, 4 * quad + 4)
                ]
                for part, value in enumerate(pack_quad(pieces)):
                    t_mine[h, :, pl.ds(quad * 384 + part * LANES, LANES)] = value.astype(jnp.bfloat16)
        for dz, dx in pushes:
            t1(j, dz, dx, True).start()

    def label(code, lead):
        irrep = jnp.bitwise_xor((code >> 7) & 7, (lead >> 7) & 7)
        return irrep + 8 * ((code >> 10) + (lead >> 10))

    picked[...] = one_hot((code_col[...] & 127) == lax.broadcasted_iota(jnp.int32, (nvir, LANES), 1))
    cd_labels = [label(code_row[...], code_s[row * c_here + c]) for c in range(c_here)]
    own = code_s[col]
    own_class = own >> 7

    def compress(n):
        load(n).wait()
        ab_label = label(code_col[pl.ds(n * rows, rows), :], own)
        pieces = []
        for c in range(c_here):
            part = v_raw[n, :, pl.ds(c * nvir, nvir)]
            masked = jnp.where(ab_label == cd_labels[c], part, jnp.zeros_like(part))
            pieces.append(nn_dot(masked, picked[...]))
        for part, value in enumerate(pack_quad(pieces)):
            packed[pl.ds(n * rows, rows), pl.ds(part * LANES, LANES)] = value.astype(jnp.bfloat16)

    def spot(code):
        return jnp.bitwise_xor(code >> 7, own_class) * SLOTS + (code & 127)

    spot_row = spot(code_row[...])

    def send_integrals(j):
        for z_ in range(RING):
            h = z_ * PER_Z + j
            index = lax.broadcasted_iota(jnp.int32, (SLOTS, nvir), 0) + h * SLOTS
            v_mine[h] = nn_dot(one_hot(spot_row == index), packed[...]).astype(jnp.bfloat16)
        for dz in (1, 3, 2, 0):
            v1(j, dz, True).start()

    def arrived(copy):
        if hasattr(copy, "wait_recv") and getattr(copy, "is_remote", True):
            copy.wait_recv()
        else:
            copy.wait()

    def multiply(j, s):
        r_mine[s, j] = nt_dot(v_all[j], t_all[s, j]).astype(jnp.bfloat16)
        for dz in (1, 3, 2, 0):
            back(j, s, dz, True).start()

    for n in range(chunks):
        compress(n)

    def round_y(j):
        for dz, dx in pushes:
            arrived(t1(j, dz, dx, False))
        t2(j, 0).start()
        t2(j, 1).start()

    def over_rows(j):
        for dz in (1, 3, 2, 0):
            arrived(v1(j, dz, False))
        v2(j, 0, True).start()
        v2(j, 1, True).start()

    def pass_on(j):
        arrived(t2(j, 0))
        t2(j, 2).start()
        arrived(t2(j, 1))
        t2(j, 3).start()

    round_y(0)
    for j in range(PER_Z):
        send_integrals(j)
        if j == 1:
            round_y(1)
    pass_on(0)
    over_rows(0)
    round_y(2)
    over_rows(1)
    pass_on(1)
    round_y(3)

    def last_row(j):
        arrived(v2(j, 1, False))
        v2(j, 2, True).start()

    def whole(j):
        arrived(v2(j, 0, False))
        arrived(v2(j, 2, False))

    over_rows(2)
    last_row(0)
    over_rows(3)
    last_row(1)
    pass_on(2)
    spot_col = spot(code_col[...])
    piece = 256
    for n in range(nvir // piece):
        column = lax.broadcasted_iota(jnp.int32, (piece, CLASSES * SLOTS), 1)
        unsort[pl.ds(n * piece, piece), :] = one_hot(spot_col[n * piece : (n + 1) * piece] == column)
    whole(0)
    for s in range(3):
        multiply(0, s)
    last_row(2)
    whole(1)
    for s in range(3):
        multiply(1, s)
    last_row(3)
    for j in (0, 1):
        arrived(t2(j, 2))
        arrived(t2(j, 3))
        multiply(j, 3)
    whole(2)
    for s in range(3):
        multiply(2, s)
    pass_on(3)
    whole(3)
    for s in range(3):
        multiply(3, s)
    for j in (2, 3):
        arrived(t2(j, 2))
        arrived(t2(j, 3))
        multiply(j, 3)

    for s in range(4):
        for j in range(PER_Z):
            for dz in range(RING):
                arrived(back(j, s, dz, False))
        lanes = pl.ds(pl.multiple_of(ring(y, (0, -1, 1, 2)[s]) * block, block), block)
        out_ref[:, lanes] = nn_dot(unsort[...], r_all[:, lanes]).astype(jnp.bfloat16)

    for j in range(PER_Z):
        for dz, dx in pushes:
            if dz or dx:
                t1(j, dz, dx, True).wait_send()
        for dz in (1, 3, 2):
            v1(j, dz, True).wait_send()
        for kind in range(3):
            v2(j, kind, True).wait_send()
        for kind in range(4):
            t2(j, kind).wait_send()
        for s in range(4):
            for dz in (1, 3, 2):
                back(j, s, dz, True).wait_send()


def blocked(code, amplitudes, integrals, orbital_irrep, orbital_spin):
    nvir = orbital_irrep.shape[0]
    pairs, cd = amplitudes.shape
    ab, cd_here = integrals.shape
    depth = (cd // nvir) * SLOTS
    width = (cd_here // nvir) * SLOTS
    block = 8 * pairs
    tall = RING * SLOTS
    rows = 128
    vmem = pl.BlockSpec(memory_space=pltpu.VMEM)
    dma = pltpu.SemaphoreType.DMA
    bf16 = jnp.bfloat16
    flipped = pl.pallas_call(
        contract,
        out_shape=jax.ShapeDtypeStruct((nvir, RING * block), bf16),
        in_specs=[pl.BlockSpec(memory_space=pltpu.SMEM), vmem, vmem, vmem, pl.BlockSpec(memory_space=pl.ANY)],
        out_specs=vmem,
        scratch_shapes=[
            pltpu.VMEM((ab // rows, rows, cd_here), bf16),
            pltpu.VMEM((cd // nvir * pairs, nvir), bf16),
            pltpu.VMEM((CLASSES, cd // nvir * pairs, LANES), jnp.float32),
            pltpu.VMEM((CLASSES, pairs, depth), bf16),
            pltpu.VMEM((nvir, LANES), bf16),
            pltpu.VMEM((ab, width), bf16),
            pltpu.VMEM((CLASSES, SLOTS, width), bf16),
            pltpu.VMEM((nvir, CLASSES * SLOTS), bf16),
            pltpu.VMEM((RING, PER_Z, block, depth), bf16),
            pltpu.VMEM((PER_Z, tall, depth), bf16),
            pltpu.VMEM((RING, PER_Z, tall, block), bf16),
            pltpu.VMEM((CLASSES * SLOTS, RING * block), bf16),
            dma((ab // rows,)),
            dma((PER_Z, 8)),
            dma((PER_Z, 8)),
            dma((PER_Z, 4)),
            dma((PER_Z, 4)),
            dma((PER_Z, 3)),
            dma((PER_Z, 3)),
            dma((PER_Z, 4)),
            dma((PER_Z, 4)),
            dma((PER_Z, 16)),
            dma((PER_Z, 16)),
        ],
        compiler_params=pltpu.CompilerParams(
            collective_id=0, has_side_effects=True, vmem_limit_bytes=56 * MIB
        ),
        name="contract",
    )(code, code[:, None], code[None, :], amplitudes, integrals)
    spread = flipped.reshape(nvir, RING, RING, 2 * pairs)
    return spread.transpose(2, 1, 3, 0).reshape(RING * block, nvir)


def local(amplitudes, integrals, orbital_irrep, orbital_spin):
    group = orbital_irrep + 8 * orbital_spin
    count = jnp.arange(group.shape[0], dtype=jnp.int32)
    earlier = (group[:, None] == group[None, :]) & (count[None, :] < count[:, None])
    rank = jnp.sum(earlier.astype(jnp.int32), axis=1)
    return lax.cond(
        jnp.max(rank) < SLOTS,
        blocked,
        lambda code, *args: dense(*args),
        group * LANES + rank,
        amplitudes,
        integrals,
        orbital_irrep,
        orbital_spin,
    )


def solution(mesh):
    placed = (P(("row", "col"), None), P("col", "row"), P(), P())
    return jax.shard_map(
        local, mesh=mesh, in_specs=placed, out_specs=P("row", "col"), check_vma=False
    )
```

```python
import functools

import jax
import jax.numpy as jnp
from jax import lax
from jax.experimental import pallas as pl
from jax.experimental.pallas import tpu as pltpu
from jax.sharding import PartitionSpec as P

MESH = pl.DeviceIdType.MESH
CLASSES = 16
SLOTS = 96
RING = 4
PER_Z = CLASSES // RING
LANES = 128
MIB = 1 << 20


def nt_dot(lhs, rhs):
    return lax.dot_general(lhs, rhs, (((1,), (1,)), ((), ())), preferred_element_type=jnp.float32)


def nn_dot(lhs, rhs):
    return jnp.dot(lhs, rhs, preferred_element_type=jnp.float32)


def pair_labels(first, count, orbital_irrep, orbital_spin):
    lead_irrep = lax.dynamic_slice_in_dim(orbital_irrep, first, count, 0)
    lead_spin = lax.dynamic_slice_in_dim(orbital_spin, first, count, 0)
    labels = jnp.bitwise_xor(lead_irrep[:, None], orbital_irrep[None, :]) + 8 * (
        lead_spin[:, None] + orbital_spin[None, :]
    )
    return labels.reshape(-1)


def dense(amplitudes, integrals, orbital_irrep, orbital_spin):
    virtuals = orbital_irrep.shape[0]
    a_count = integrals.shape[0] // virtuals
    c_count = integrals.shape[1] // virtuals
    ab_labels = pair_labels(lax.axis_index("col") * a_count, a_count, orbital_irrep, orbital_spin)
    cd_labels = pair_labels(lax.axis_index("row") * c_count, c_count, orbital_irrep, orbital_spin)
    masked = jnp.where(
        ab_labels[:, None] == cd_labels[None, :], integrals, jnp.zeros((), integrals.dtype)
    )
    grid_rows = lax.all_gather(amplitudes, "col", axis=0, tiled=True)
    regrouped = lax.all_to_all(grid_rows, "row", split_axis=1, concat_axis=0, tiled=True)
    partial_sums = nt_dot(regrouped, masked)
    return lax.psum_scatter(partial_sums, "row", scatter_dimension=0, tiled=True).astype(
        jnp.bfloat16
    )


def one_hot(hit):
    return jnp.where(hit, 1.0, 0.0).astype(jnp.bfloat16)


def pack_quad(pieces):
    first, second, third, fourth = pieces
    lane = lax.broadcasted_iota(jnp.int32, first.shape, 1)
    zero = jnp.zeros_like(first)
    second = pltpu.roll(second, 96, 1)
    third = pltpu.roll(third, 64, 1)
    fourth = pltpu.roll(fourth, 32, 1)
    return (
        first + jnp.where(lane >= 96, second, zero),
        jnp.where(lane < 64, second, zero) + jnp.where(lane >= 64, third, zero),
        jnp.where(lane < 32, third, zero) + fourth,
    )


def contract(
    code_s, code_col, code_row, t_ref, v_hbm, out_ref,
    v_raw, stacked, by_class, t_mine, picked, packed, v_mine, unsort, t_all, v_all, r_mine, r_all,
    loads, t1s, t1r, v1s, v1r, v2s, v2r, t2s, t2r, rs, rr,
):
    row, col = lax.axis_index("row"), lax.axis_index("col")
    z, y, xl = col // 8, (col // 2) % 4, col % 2
    nvir = code_col.shape[0]
    pairs, c_tot = t_ref.shape[0], t_ref.shape[1] // nvir
    c_here = v_hbm.shape[1] // nvir
    block = 8 * pairs
    width = c_here * SLOTS
    chunks, rows = v_raw.shape[0], v_raw.shape[1]

    def load(n):
        return pltpu.make_async_copy(v_hbm.at[pl.ds(n * rows, rows), :], v_raw.at[n], loads.at[n])

    for n in range(chunks):
        load(n).start()

    def place(z_, y_, xl_):
        return z_ * 8 + y_ * 2 + xl_

    def ring(value, shift):
        return lax.rem(value + (shift + RING), RING)

    core_row = jnp.bitwise_xor(row, 1)
    far_row = ring(row, 2)

    def remote(src, dst, send, recv, row_, col_):
        return pltpu.make_async_remote_copy(
            src_ref=src, dst_ref=dst, send_sem=send, recv_sem=recv, device_id=(row_, col_), device_id_type=MESH
        )

    def t1(j, dz, dx, sending):
        to_z, to_x = ring(z, dz), jnp.bitwise_xor(xl, dx)
        from_z = z if sending else ring(z, -dz)
        from_x = xl if sending else to_x
        here = pl.multiple_of((from_z * 2 + from_x) * pairs, pairs)
        src = t_mine.at[to_z * PER_Z + j]
        dst = t_all.at[0, j, pl.ds(here, pairs), :]
        if dz == 0 and dx == 0:
            return pltpu.make_async_copy(src, dst, t1r.at[j, 0])
        n = dz * 2 + dx
        return remote(src, dst, t1s.at[j, n], t1r.at[j, n], row, place(to_z, y, to_x))

    def v1(j, dz, sending):
        to_z = ring(z, dz)
        from_z = z if sending else ring(z, -dz)
        src = v_mine.at[j, pl.ds(pl.multiple_of(to_z * SLOTS, SLOTS), SLOTS), :]
        dst = v_all.at[
            j, pl.ds(pl.multiple_of(from_z * SLOTS, SLOTS), SLOTS), pl.ds(pl.multiple_of(row * width, width), width)
        ]
        if dz == 0:
            return pltpu.make_async_copy(src, dst, v1r.at[j, 0])
        return remote(src, dst, v1s.at[j, dz], v1r.at[j, dz], row, place(to_z, y, xl))

    def v2(j, kind, sending):
        if kind == 0:
            of = row if sending else core_row
        elif kind == 1:
            of = row if sending else far_row
        else:
            of = far_row if sending else ring(core_row, 2)
        part = v_all.at[j, :, pl.ds(pl.multiple_of(of * width, width), width)]
        return remote(part, part, v2s.at[j, kind], v2r.at[j, kind], far_row if kind == 1 else core_row, col)

    def t2(j, kind):
        half = block // 2
        up, down = place(z, ring(y, 1), xl), place(z, ring(y, -1), xl)
        if kind == 0:
            src, dst, to = t_all.at[0, j], t_all.at[1, j], up
        elif kind == 1:
            src, dst, to = t_all.at[0, j], t_all.at[2, j], down
        elif kind == 2:
            src, dst, to = t_all.at[1, j, pl.ds(0, half), :], t_all.at[3, j, pl.ds(0, half), :], up
        else:
            src, dst, to = t_all.at[2, j, pl.ds(half, half), :], t_all.at[3, j, pl.ds(half, half), :], down
        return remote(src, dst, t2s.at[j, kind], t2r.at[j, kind], row, to)

    def back(j, s, dz, sending):
        to_z = ring(z, dz)
        from_z = z if sending else ring(z, -dz)
        y_of = ring(y, (0, -1, 1, 2)[s])
        src = r_mine.at[s, j, pl.ds(pl.multiple_of(to_z * SLOTS, SLOTS), SLOTS), :]
        dst = r_all.at[
            pl.ds(pl.multiple_of((from_z * PER_Z + j) * SLOTS, SLOTS), SLOTS),
            pl.ds(pl.multiple_of(y_of * block, block), block),
        ]
        n = s * RING + dz
        if dz == 0:
            return pltpu.make_async_copy(src, dst, rr.at[j, n])
        return remote(src, dst, rs.at[j, n], rr.at[j, n], row, place(to_z, y, xl))

    pushes = [(dz, dx) for dz in (1, 3, 2, 0) for dx in (0, 1)]

    barrier = pltpu.get_barrier_semaphore()
    peers = [(row, place(ring(z, dz), y, jnp.bitwise_xor(xl, dx))) for dz, dx in pushes if dz or dx]
    peers += [(row, place(z, ring(y, 1), xl)), (row, place(z, ring(y, -1), xl)), (core_row, col), (far_row, col)]
    for peer in peers:
        pl.semaphore_signal(barrier, inc=1, device_id=peer, device_id_type=MESH)

    def sort():
        for c in range(c_tot):
            stacked[pl.ds(c * pairs, pairs), :] = t_ref[:, pl.ds(c * nvir, nvir)]
        for pair in range(CLASSES // 2):
            column = lax.broadcasted_iota(jnp.int32, (nvir, 2 * LANES), 1) + pair * 2 * LANES
            got = nn_dot(stacked[...], one_hot(code_col[...] == column))
            by_class[2 * pair] = got[:, :LANES]
            by_class[2 * pair + 1] = got[:, LANES:]

    classes = [code_s[c] >> 7 for c in range(c_tot)]

    def arrange(j):
        for z_ in range(RING):
            h = z_ * PER_Z + j
            for quad in range(c_tot // 4):
                pieces = [
                    by_class[jnp.bitwise_xor(classes[c], h), pl.ds(c * pairs, pairs), :]
                    for c in range(4 * quad, 4 * quad + 4)
                ]
                for part, value in enumerate(pack_quad(pieces)):
                    t_mine[h, :, pl.ds(quad * 384 + part * LANES, LANES)] = value.astype(jnp.bfloat16)

    def label(code, lead):
        irrep = jnp.bitwise_xor((code >> 7) & 7, (lead >> 7) & 7)
        return irrep + 8 * ((code >> 10) + (lead >> 10))

    cd_labels = [label(code_row[...], code_s[row * c_here + c]) for c in range(c_here)]
    own = code_s[col]

    def spot(code):
        return jnp.bitwise_xor(code >> 7, own >> 7) * SLOTS + (code & 127)

    spot_row = spot(code_row[...])

    def compress(n):
        load(n).wait()
        ab_label = label(code_col[pl.ds(n * rows, rows), :], own)
        pieces = []
        for c in range(c_here):
            part = v_raw[n, :, pl.ds(c * nvir, nvir)]
            masked = jnp.where(ab_label == cd_labels[c], part, jnp.zeros_like(part))
            pieces.append(nn_dot(masked, picked[...]))
        for part, value in enumerate(pack_quad(pieces)):
            packed[pl.ds(n * rows, rows), pl.ds(part * LANES, LANES)] = value.astype(jnp.bfloat16)

    def permute(j):
        line = lax.broadcasted_iota(jnp.int32, (RING * SLOTS, nvir), 0)
        over = sum((line >= z_ * SLOTS).astype(jnp.int32) for z_ in range(1, RING))
        index = line + over * ((PER_Z - 1) * SLOTS) + j * SLOTS
        v_mine[j] = nn_dot(one_hot(spot_row == index), packed[...]).astype(jnp.bfloat16)

    def build_unsort(n):
        piece = nvir // PER_Z
        where = spot(code_col[pl.ds(n * piece, piece), :])
        column = lax.broadcasted_iota(jnp.int32, (piece, CLASSES * SLOTS), 1)
        unsort[pl.ds(n * piece, piece), :] = one_hot(where == column)

    def arrived(copy):
        if copy.is_remote:
            copy.wait_recv()
        else:
            copy.wait()

    def send_amplitudes(j):
        arrange(j)
        for dz, dx in pushes:
            t1(j, dz, dx, True).start()

    def send_integrals(j):
        permute(j)
        for dz in (1, 3, 2, 0):
            v1(j, dz, True).start()

    def round_y(j):
        for dz, dx in pushes:
            arrived(t1(j, dz, dx, False))
        t2(j, 0).start()
        t2(j, 1).start()

    def pass_on(j):
        arrived(t2(j, 0))
        t2(j, 2).start()
        arrived(t2(j, 1))
        t2(j, 3).start()

    def over_rows(j):
        for dz in (1, 3, 2, 0):
            arrived(v1(j, dz, False))
        v2(j, 0, True).start()
        v2(j, 1, True).start()

    def last_row(j):
        arrived(v2(j, 1, False))
        v2(j, 2, True).start()

    def multiply(j, s):
        r_mine[s, j] = nt_dot(v_all[j], t_all[s, j]).astype(jnp.bfloat16)
        for dz in (1, 3, 2, 0):
            back(j, s, dz, True).start()

    def near(j):
        arrived(v2(j, 0, False))
        arrived(v2(j, 2, False))
        for s in range(3):
            multiply(j, s)

    def far(j):
        arrived(t2(j, 2))
        arrived(t2(j, 3))
        multiply(j, 3)

    def finish(s):
        for j in range(PER_Z):
            for dz in range(RING):
                arrived(back(j, s, dz, False))
        lanes = pl.ds(pl.multiple_of(ring(y, (0, -1, 1, 2)[s]) * block, block), block)
        out_ref[:, lanes] = nn_dot(unsort[...], r_all[:, lanes]).astype(jnp.bfloat16)

    sort()
    pl.semaphore_wait(barrier, len(peers))
    for j in range(PER_Z):
        send_amplitudes(j)
    picked[...] = one_hot((code_col[...] & 127) == lax.broadcasted_iota(jnp.int32, (nvir, LANES), 1))
    for n in range(chunks):
        compress(n)
        if n == chunks // 2:
            round_y(0)
    send_integrals(0)
    send_integrals(1)
    round_y(1)
    send_integrals(2)
    send_integrals(3)
    pass_on(0)
    over_rows(0)
    round_y(2)
    over_rows(1)
    pass_on(1)
    round_y(3)
    last_row(0)
    over_rows(2)
    last_row(1)
    over_rows(3)
    build_unsort(0)
    build_unsort(1)
    near(0)
    pass_on(2)
    last_row(2)
    near(1)
    far(0)
    last_row(3)
    build_unsort(2)
    build_unsort(3)
    pass_on(3)
    far(1)
    near(2)
    far(2)
    near(3)
    finish(0)
    far(3)
    for s in range(1, 4):
        finish(s)

    for j in range(PER_Z):
        for dz, dx in pushes:
            if dz or dx:
                t1(j, dz, dx, True).wait_send()
        for dz in (1, 3, 2):
            v1(j, dz, True).wait_send()
        for kind in range(3):
            v2(j, kind, True).wait_send()
        for kind in range(4):
            t2(j, kind).wait_send()
        for s in range(4):
            for dz in (1, 3, 2):
                back(j, s, dz, True).wait_send()


def blocked(code, amplitudes, integrals, orbital_irrep, orbital_spin):
    nvir = orbital_irrep.shape[0]
    pairs, cd = amplitudes.shape
    ab, cd_here = integrals.shape
    depth = (cd // nvir) * SLOTS
    width = (cd_here // nvir) * SLOTS
    block = 8 * pairs
    tall = RING * SLOTS
    rows = 128
    vmem = pl.BlockSpec(memory_space=pltpu.VMEM)
    dma = pltpu.SemaphoreType.DMA
    bf16 = jnp.bfloat16
    flipped = pl.pallas_call(
        contract,
        out_shape=jax.ShapeDtypeStruct((nvir, RING * block), bf16),
        in_specs=[pl.BlockSpec(memory_space=pltpu.SMEM), vmem, vmem, vmem, pl.BlockSpec(memory_space=pl.ANY)],
        out_specs=vmem,
        scratch_shapes=[
            pltpu.VMEM((ab // rows, rows, cd_here), bf16),
            pltpu.VMEM((cd // nvir * pairs, nvir), bf16),
            pltpu.VMEM((CLASSES, cd // nvir * pairs, LANES), jnp.float32),
            pltpu.VMEM((CLASSES, pairs, depth), bf16),
            pltpu.VMEM((nvir, LANES), bf16),
            pltpu.VMEM((ab, width), bf16),
            pltpu.VMEM((PER_Z, tall, width), bf16),
            pltpu.VMEM((nvir, CLASSES * SLOTS), bf16),
            pltpu.VMEM((RING, PER_Z, block, depth), bf16),
            pltpu.VMEM((PER_Z, tall, depth), bf16),
            pltpu.VMEM((RING, PER_Z, tall, block), bf16),
            pltpu.VMEM((CLASSES * SLOTS, RING * block), bf16),
            dma((ab // rows,)),
            dma((PER_Z, 8)),
            dma((PER_Z, 8)),
            dma((PER_Z, 4)),
            dma((PER_Z, 4)),
            dma((PER_Z, 3)),
            dma((PER_Z, 3)),
            dma((PER_Z, 4)),
            dma((PER_Z, 4)),
            dma((PER_Z, 16)),
            dma((PER_Z, 16)),
        ],
        compiler_params=pltpu.CompilerParams(
            collective_id=0, has_side_effects=True, vmem_limit_bytes=38 * MIB
        ),
        name="contract",
    )(code, code[:, None], code[None, :], amplitudes, integrals)
    spread = flipped.reshape(nvir, RING, RING, 2 * pairs)
    return spread.transpose(2, 1, 3, 0).reshape(RING * block, nvir)


def local(amplitudes, integrals, orbital_irrep, orbital_spin):
    group = orbital_irrep + 8 * orbital_spin
    count = jnp.arange(group.shape[0], dtype=jnp.int32)
    earlier = (group[:, None] == group[None, :]) & (count[None, :] < count[:, None])
    rank = jnp.sum(earlier.astype(jnp.int32), axis=1)
    return lax.cond(
        jnp.max(rank) < SLOTS,
        blocked,
        lambda code, *args: dense(*args),
        group * LANES + rank,
        amplitudes,
        integrals,
        orbital_irrep,
        orbital_spin,
    )


def solution(mesh):
    placed = (P(("row", "col"), None), P("col", "row"), P(), P())
    return jax.shard_map(
        local, mesh=mesh, in_specs=placed, out_specs=P("row", "col"), check_vma=False
    )
```

```python
import functools

import jax
import jax.numpy as jnp
from jax import lax
from jax.experimental import pallas as pl
from jax.experimental.pallas import tpu as pltpu
from jax.sharding import PartitionSpec as P

MESH = pl.DeviceIdType.MESH
CLASSES = 16
SLOTS = 96
RING = 4
PER_OWNER = CLASSES // RING
ORDER = (1, 3, 2, 0)
SHIFT = (0, -1, 1, 2)
LANES = 128
MIB = 1 << 20


def nt_dot(lhs, rhs):
    return lax.dot_general(lhs, rhs, (((1,), (1,)), ((), ())), preferred_element_type=jnp.float32)


def nn_dot(lhs, rhs):
    return jnp.dot(lhs, rhs, preferred_element_type=jnp.float32)


def tn_dot(lhs, rhs):
    return lax.dot_general(lhs, rhs, (((0,), (0,)), ((), ())), preferred_element_type=jnp.float32)


def pair_labels(first, count, orbital_irrep, orbital_spin):
    lead_irrep = lax.dynamic_slice_in_dim(orbital_irrep, first, count, 0)
    lead_spin = lax.dynamic_slice_in_dim(orbital_spin, first, count, 0)
    labels = jnp.bitwise_xor(lead_irrep[:, None], orbital_irrep[None, :]) + 8 * (
        lead_spin[:, None] + orbital_spin[None, :]
    )
    return labels.reshape(-1)


def dense(amplitudes, integrals, orbital_irrep, orbital_spin):
    virtuals = orbital_irrep.shape[0]
    a_count = integrals.shape[0] // virtuals
    c_count = integrals.shape[1] // virtuals
    ab_labels = pair_labels(lax.axis_index("col") * a_count, a_count, orbital_irrep, orbital_spin)
    cd_labels = pair_labels(lax.axis_index("row") * c_count, c_count, orbital_irrep, orbital_spin)
    masked = jnp.where(
        ab_labels[:, None] == cd_labels[None, :], integrals, jnp.zeros((), integrals.dtype)
    )
    grid_rows = lax.all_gather(amplitudes, "col", axis=0, tiled=True)
    regrouped = lax.all_to_all(grid_rows, "row", split_axis=1, concat_axis=0, tiled=True)
    partial_sums = nt_dot(regrouped, masked)
    return lax.psum_scatter(partial_sums, "row", scatter_dimension=0, tiled=True).astype(
        jnp.bfloat16
    )


def one_hot(hit):
    return jnp.where(hit, 1.0, 0.0).astype(jnp.bfloat16)


def pack_quad(pieces):
    first, second, third, fourth = pieces
    lane = lax.broadcasted_iota(jnp.int32, first.shape, 1)
    zero = jnp.zeros_like(first)
    second = pltpu.roll(second, 96, 1)
    third = pltpu.roll(third, 64, 1)
    fourth = pltpu.roll(fourth, 32, 1)
    return (
        first + jnp.where(lane >= 96, second, zero),
        jnp.where(lane < 64, second, zero) + jnp.where(lane >= 64, third, zero),
        jnp.where(lane < 32, third, zero) + fourth,
    )


def contract(
    code_s, code_col, code_row, t_ref, v_hbm, out_ref,
    v_raw, stacked, by_class, t_mine, picked, packed, v_mine, unsort, t_all, v_all, r_mine, r_all,
    loads, t1s, t1r, xs, xr, v1s, v1r, v2s, v2r, t2s, t2r, rs, rr,
):
    row, col = lax.axis_index("row"), lax.axis_index("col")
    z, y, xl = col // 8, (col // 2) % 4, col % 2
    nvir = code_col.shape[0]
    pairs, c_tot = t_ref.shape[0], t_ref.shape[1] // nvir
    c_here = v_hbm.shape[1] // nvir
    block = 8 * pairs
    width = c_here * SLOTS
    chunks, rows = v_raw.shape[0], v_raw.shape[1]

    def load(n):
        return pltpu.make_async_copy(v_hbm.at[pl.ds(n * rows, rows), :], v_raw.at[n], loads.at[n])

    for n in range(chunks):
        load(n).start()

    def ring(value, shift):
        return lax.rem(value + (shift + RING), RING)

    def axes(j):
        return (z, y) if j % 2 == 0 else (y, z)

    def place(j, owner, along, xl_=xl):
        z_, y_ = (owner, along) if j % 2 == 0 else (along, owner)
        return z_ * 8 + y_ * 2 + xl_

    core_row = jnp.bitwise_xor(row, 1)
    far_row = ring(row, 2)

    def remote(src, dst, send, recv, row_, col_):
        return pltpu.make_async_remote_copy(
            src_ref=src, dst_ref=dst, send_sem=send, recv_sem=recv, device_id=(row_, col_), device_id_type=MESH
        )

    def t1(j, shift, sending):
        owner, along = axes(j)
        to = ring(owner, shift)
        source = owner if sending else ring(owner, -shift)
        src = t_mine.at[to * PER_OWNER + j]
        dst = t_all.at[0, j, pl.ds(pl.multiple_of((xl * RING + source) * pairs, pairs), pairs), :]
        if shift == 0:
            return pltpu.make_async_copy(src, dst, t1r.at[j, 0])
        return remote(src, dst, t1s.at[j, shift], t1r.at[j, shift], row, place(j, to, along))

    def half(e):
        return pl.ds(pl.multiple_of(jnp.bitwise_xor(xl, e) * (block // 2), block // 2), block // 2)

    def cross(j, sending):
        part = t_all.at[0, j, half(0 if sending else 1), :]
        return remote(part, part, xs.at[j], xr.at[j], row, jnp.bitwise_xor(col, 1))

    def v1(j, shift, sending):
        owner, along = axes(j)
        to = ring(owner, shift)
        source = owner if sending else ring(owner, -shift)
        src = v_mine.at[j, pl.ds(pl.multiple_of(to * SLOTS, SLOTS), SLOTS), :]
        dst = v_all.at[
            j, pl.ds(pl.multiple_of(source * SLOTS, SLOTS), SLOTS), pl.ds(pl.multiple_of(row * width, width), width)
        ]
        if shift == 0:
            return pltpu.make_async_copy(src, dst, v1r.at[j, 0])
        return remote(src, dst, v1s.at[j, shift], v1r.at[j, shift], row, place(j, to, along))

    def v2(j, kind, sending):
        if kind == 0:
            of = row if sending else core_row
        elif kind == 1:
            of = row if sending else far_row
        else:
            of = far_row if sending else ring(core_row, 2)
        part = v_all.at[j, :, pl.ds(pl.multiple_of(of * width, width), width)]
        return remote(part, part, v2s.at[j, kind], v2r.at[j, kind], far_row if kind == 1 else core_row, col)

    def t2(j, kind):
        owner, along = axes(j)
        e = kind % 2
        up = kind in (0, 1, 4)
        from_slot, to_slot = ((0, 1) if up else (0, 2)) if kind < 4 else ((1, 3) if up else (2, 3))
        src, dst = t_all.at[from_slot, j, half(e), :], t_all.at[to_slot, j, half(e), :]
        return remote(
            src, dst, t2s.at[j, kind], t2r.at[j, kind], row, place(j, owner, ring(along, 1 if up else -1))
        )

    def back(j, s, shift, sending):
        owner, along = axes(j)
        to = ring(owner, shift)
        source = owner if sending else ring(owner, -shift)
        src = r_mine.at[s, j, pl.ds(pl.multiple_of(to * SLOTS, SLOTS), SLOTS), :]
        dst = r_all.at[
            j % 2,
            pl.ds(pl.multiple_of((source * 2 + j // 2) * SLOTS, SLOTS), SLOTS),
            pl.ds(pl.multiple_of(ring(along, SHIFT[s]) * block, block), block),
        ]
        n = s * RING + shift
        if shift == 0:
            return pltpu.make_async_copy(src, dst, rr.at[j, n])
        return remote(src, dst, rs.at[j, n], rr.at[j, n], row, place(j, to, along))

    barrier = pltpu.get_barrier_semaphore()
    peers = [(row, place(j, ring(axes(j)[0], shift), axes(j)[1])) for j in (0, 1) for shift in (1, 3, 2)]
    peers += [(row, jnp.bitwise_xor(col, 1)), (core_row, col), (far_row, col)]
    for peer in peers:
        pl.semaphore_signal(barrier, inc=1, device_id=peer, device_id_type=MESH)

    def sort():
        for c in range(c_tot):
            stacked[pl.ds(c * pairs, pairs), :] = t_ref[:, pl.ds(c * nvir, nvir)]
        for pair in range(CLASSES // 2):
            column = lax.broadcasted_iota(jnp.int32, (nvir, 2 * LANES), 1) + pair * 2 * LANES
            got = nn_dot(stacked[...], one_hot(code_col[...] == column))
            by_class[2 * pair] = got[:, :LANES]
            by_class[2 * pair + 1] = got[:, LANES:]

    classes = [code_s[c] >> 7 for c in range(c_tot)]

    def arrange(j):
        for z_ in range(RING):
            h = z_ * PER_OWNER + j
            for quad in range(c_tot // 4):
                pieces = [
                    by_class[jnp.bitwise_xor(classes[c], h), pl.ds(c * pairs, pairs), :]
                    for c in range(4 * quad, 4 * quad + 4)
                ]
                for part, value in enumerate(pack_quad(pieces)):
                    t_mine[h, :, pl.ds(quad * 384 + part * LANES, LANES)] = value.astype(jnp.bfloat16)

    def label(code, lead):
        irrep = jnp.bitwise_xor((code >> 7) & 7, (lead >> 7) & 7)
        return irrep + 8 * ((code >> 10) + (lead >> 10))

    cd_labels = [label(code_row[...], code_s[row * c_here + c]) for c in range(c_here)]
    own = code_s[col]

    def spot(code):
        return jnp.bitwise_xor(code >> 7, own >> 7) * SLOTS + (code & 127)

    spot_row = spot(code_row[...])

    def compress(n):
        load(n).wait()
        ab_label = label(code_col[pl.ds(n * rows, rows), :], own)
        pieces = []
        for c in range(c_here):
            part = v_raw[n, :, pl.ds(c * nvir, nvir)]
            masked = jnp.where(ab_label == cd_labels[c], part, jnp.zeros_like(part))
            pieces.append(nn_dot(masked, picked[...]))
        for part, value in enumerate(pack_quad(pieces)):
            packed[pl.ds(n * rows, rows), pl.ds(part * LANES, LANES)] = value.astype(jnp.bfloat16)

    def permute(j):
        line = lax.broadcasted_iota(jnp.int32, (RING * SLOTS, nvir), 0)
        over = sum((line >= z_ * SLOTS).astype(jnp.int32) for z_ in range(1, RING))
        index = line + over * ((PER_OWNER - 1) * SLOTS) + j * SLOTS
        v_mine[j] = nn_dot(one_hot(spot_row == index), packed[...]).astype(jnp.bfloat16)

    def build_unsort(parity):
        h = jnp.bitwise_xor(code_row[...] >> 7, own >> 7)
        line = ((h >> 2) * 2 + ((h >> 1) & 1)) * SLOTS + (code_row[...] & 127)
        line = jnp.where((h & 1) == parity, line, -1)
        index = lax.broadcasted_iota(jnp.int32, unsort.shape[1:], 0)
        unsort[parity] = one_hot(line == index)

    def arrived(copy):
        if copy.is_remote:
            copy.wait_recv()
        else:
            copy.wait()

    def send_amplitudes(j):
        arrange(j)
        for shift in ORDER:
            t1(j, shift, True).start()

    def send_integrals(j):
        permute(j)
        for shift in ORDER:
            v1(j, shift, True).start()

    def begin_ring(j):
        for shift in ORDER:
            arrived(t1(j, shift, False))
        cross(j, True).start()
        t2(j, 0).start()
        t2(j, 2).start()

    def join_ring(j):
        arrived(cross(j, False))
        t2(j, 1).start()
        t2(j, 3).start()

    def pass_on(j):
        arrived(t2(j, 0))
        t2(j, 4).start()
        arrived(t2(j, 3))
        t2(j, 5).start()

    def over_rows(j):
        for shift in ORDER:
            arrived(v1(j, shift, False))
        v2(j, 0, True).start()
        v2(j, 1, True).start()

    def last_row(j):
        arrived(v2(j, 1, False))
        v2(j, 2, True).start()

    def multiply(j, s):
        r_mine[s, j] = nt_dot(v_all[j], t_all[s, j]).astype(jnp.bfloat16)
        for shift in ORDER:
            back(j, s, shift, True).start()

    def near(j):
        arrived(v2(j, 0, False))
        arrived(v2(j, 2, False))
        multiply(j, 0)
        arrived(t2(j, 1))
        multiply(j, 1)
        arrived(t2(j, 2))
        multiply(j, 2)

    def far(j):
        arrived(t2(j, 4))
        arrived(t2(j, 5))
        multiply(j, 3)

    def finish(parity, s):
        for j in (parity, parity + 2):
            for shift in range(RING):
                arrived(back(j, s, shift, False))
        along = ring(axes(parity)[1], SHIFT[s])
        lanes = pl.ds(pl.multiple_of(along * block, block), block)
        got = tn_dot(r_all[parity, :, lanes], unsort[parity]).astype(jnp.bfloat16)
        for n in range(8):
            xl_, other = n // RING, n % RING
            z_, y_ = (other, along) if parity == 0 else (along, other)
            at = pl.ds(pl.multiple_of(z_ * block + (y_ * 2 + xl_) * pairs, pairs), pairs)
            piece = got[n * pairs : (n + 1) * pairs]
            out_ref[at, :] = piece if parity == 0 else out_ref[at, :] + piece

    sort()
    pl.semaphore_wait(barrier, len(peers))
    for j in range(PER_OWNER):
        send_amplitudes(j)
    picked[...] = one_hot((code_col[...] & 127) == lax.broadcasted_iota(jnp.int32, (nvir, LANES), 1))
    for n in range(chunks):
        compress(n)
        if n == 3:
            begin_ring(0)
        if n == 5:
            begin_ring(1)
            join_ring(0)
    join_ring(1)
    send_integrals(0)
    begin_ring(2)
    send_integrals(1)
    begin_ring(3)
    send_integrals(2)
    join_ring(2)
    send_integrals(3)
    join_ring(3)
    over_rows(0)
    pass_on(0)
    over_rows(1)
    pass_on(1)
    last_row(0)
    over_rows(2)
    last_row(1)
    over_rows(3)
    build_unsort(0)
    near(0)
    pass_on(2)
    last_row(2)
    near(1)
    far(0)
    pass_on(3)
    last_row(3)
    build_unsort(1)
    far(1)
    near(2)
    near(3)
    far(2)
    finish(0, 0)
    far(3)
    for s in range(1, 4):
        finish(0, s)
    for s in range(4):
        finish(1, s)

    for j in range(PER_OWNER):
        for shift in range(1, RING):
            t1(j, shift, True).wait_send()
            v1(j, shift, True).wait_send()
        cross(j, True).wait_send()
        for kind in range(3):
            v2(j, kind, True).wait_send()
        for kind in range(6):
            t2(j, kind).wait_send()
        for s in range(4):
            for shift in range(1, RING):
                back(j, s, shift, True).wait_send()


def blocked(code, amplitudes, integrals, orbital_irrep, orbital_spin):
    nvir = orbital_irrep.shape[0]
    pairs, cd = amplitudes.shape
    ab, cd_here = integrals.shape
    depth = (cd // nvir) * SLOTS
    width = (cd_here // nvir) * SLOTS
    block = 8 * pairs
    tall = RING * SLOTS
    rows = 128
    vmem = pl.BlockSpec(memory_space=pltpu.VMEM)
    dma = pltpu.SemaphoreType.DMA
    bf16 = jnp.bfloat16
    return pl.pallas_call(
        contract,
        out_shape=jax.ShapeDtypeStruct((RING * block, nvir), bf16),
        in_specs=[pl.BlockSpec(memory_space=pltpu.SMEM), vmem, vmem, vmem, pl.BlockSpec(memory_space=pl.ANY)],
        out_specs=vmem,
        scratch_shapes=[
            pltpu.VMEM((ab // rows, rows, cd_here), bf16),
            pltpu.VMEM((cd // nvir * pairs, nvir), bf16),
            pltpu.VMEM((CLASSES, cd // nvir * pairs, LANES), jnp.float32),
            pltpu.VMEM((CLASSES, pairs, depth), bf16),
            pltpu.VMEM((nvir, LANES), bf16),
            pltpu.VMEM((ab, width), bf16),
            pltpu.VMEM((PER_OWNER, tall, width), bf16),
            pltpu.VMEM((2, CLASSES // 2 * SLOTS, nvir), bf16),
            pltpu.VMEM((RING, PER_OWNER, block, depth), bf16),
            pltpu.VMEM((PER_OWNER, tall, depth), bf16),
            pltpu.VMEM((RING, PER_OWNER, tall, block), bf16),
            pltpu.VMEM((2, CLASSES // 2 * SLOTS, RING * block), bf16),
            dma((ab // rows,)),
            *[dma((PER_OWNER, 4))] * 2,
            *[dma((PER_OWNER,))] * 2,
            *[dma((PER_OWNER, 4))] * 2,
            *[dma((PER_OWNER, 3))] * 2,
            *[dma((PER_OWNER, 6))] * 2,
            *[dma((PER_OWNER, 16))] * 2,
        ],
        compiler_params=pltpu.CompilerParams(
            collective_id=0, has_side_effects=True, vmem_limit_bytes=38 * MIB
        ),
        name="contract",
    )(code, code[:, None], code[None, :], amplitudes, integrals)


def local(amplitudes, integrals, orbital_irrep, orbital_spin):
    group = orbital_irrep + 8 * orbital_spin
    count = jnp.arange(group.shape[0], dtype=jnp.int32)
    earlier = (group[:, None] == group[None, :]) & (count[None, :] < count[:, None])
    rank = jnp.sum(earlier.astype(jnp.int32), axis=1)
    return lax.cond(
        jnp.max(rank) < SLOTS,
        blocked,
        lambda code, *args: dense(*args),
        group * LANES + rank,
        amplitudes,
        integrals,
        orbital_irrep,
        orbital_spin,
    )


def solution(mesh):
    placed = (P(("row", "col"), None), P("col", "row"), P(), P())
    return jax.shard_map(
        local, mesh=mesh, in_specs=placed, out_specs=P("row", "col"), check_vma=False
    )
```

```python
import functools

import jax
import jax.numpy as jnp
from jax import lax
from jax.experimental import pallas as pl
from jax.experimental.pallas import tpu as pltpu
from jax.sharding import PartitionSpec as P

MESH = pl.DeviceIdType.MESH
CLASSES = 16
SLOTS = 96
RING = 4
PER_OWNER = CLASSES // RING
ORDER = (1, 3, 2, 0)
SHIFT = (0, -1, 1, 2)
LANES = 128
MIB = 1 << 20


def nt_dot(lhs, rhs):
    return lax.dot_general(lhs, rhs, (((1,), (1,)), ((), ())), preferred_element_type=jnp.float32)


def nn_dot(lhs, rhs):
    return jnp.dot(lhs, rhs, preferred_element_type=jnp.float32)


def tn_dot(lhs, rhs):
    return lax.dot_general(lhs, rhs, (((0,), (0,)), ((), ())), preferred_element_type=jnp.float32)


def pair_labels(first, count, orbital_irrep, orbital_spin):
    lead_irrep = lax.dynamic_slice_in_dim(orbital_irrep, first, count, 0)
    lead_spin = lax.dynamic_slice_in_dim(orbital_spin, first, count, 0)
    labels = jnp.bitwise_xor(lead_irrep[:, None], orbital_irrep[None, :]) + 8 * (
        lead_spin[:, None] + orbital_spin[None, :]
    )
    return labels.reshape(-1)


def dense(amplitudes, integrals, orbital_irrep, orbital_spin):
    virtuals = orbital_irrep.shape[0]
    a_count = integrals.shape[0] // virtuals
    c_count = integrals.shape[1] // virtuals
    ab_labels = pair_labels(lax.axis_index("col") * a_count, a_count, orbital_irrep, orbital_spin)
    cd_labels = pair_labels(lax.axis_index("row") * c_count, c_count, orbital_irrep, orbital_spin)
    masked = jnp.where(
        ab_labels[:, None] == cd_labels[None, :], integrals, jnp.zeros((), integrals.dtype)
    )
    grid_rows = lax.all_gather(amplitudes, "col", axis=0, tiled=True)
    regrouped = lax.all_to_all(grid_rows, "row", split_axis=1, concat_axis=0, tiled=True)
    partial_sums = nt_dot(regrouped, masked)
    return lax.psum_scatter(partial_sums, "row", scatter_dimension=0, tiled=True).astype(
        jnp.bfloat16
    )


def one_hot(hit):
    return jnp.where(hit, 1.0, 0.0).astype(jnp.bfloat16)


def pack_quad(pieces):
    first, second, third, fourth = pieces
    lane = lax.broadcasted_iota(jnp.int32, first.shape, 1)
    zero = jnp.zeros_like(first)
    second = pltpu.roll(second, 96, 1)
    third = pltpu.roll(third, 64, 1)
    fourth = pltpu.roll(fourth, 32, 1)
    return (
        first + jnp.where(lane >= 96, second, zero),
        jnp.where(lane < 64, second, zero) + jnp.where(lane >= 64, third, zero),
        jnp.where(lane < 32, third, zero) + fourth,
    )


def contract(
    code_s, code_col, code_row, t_ref, v_hbm, out_ref,
    v_raw, t_other, stacked, by_class, t_mine, picked, packed, v_mine, unsort, t_all, v_all, r_mine, r_all,
    loads, t1s, t1r, xs, xr, v1s, v1r, v2s, v2r, t2s, t2r, rs, rr,
):
    row, col = lax.axis_index("row"), lax.axis_index("col")
    z, y, xl = col // 8, (col // 2) % 4, col % 2
    nvir = code_col.shape[0]
    pairs, c_tot = t_ref.shape[0], t_ref.shape[1] // nvir
    c_here = v_hbm.shape[1] // nvir
    block = 8 * pairs
    width = c_here * SLOTS
    chunks, rows = v_raw.shape[0], v_raw.shape[1]

    def load(n):
        return pltpu.make_async_copy(v_hbm.at[pl.ds(n * rows, rows), :], v_raw.at[n], loads.at[n])

    for n in range(chunks):
        load(n).start()

    def ring(value, shift):
        return lax.rem(value + (shift + RING), RING)

    def axes(j):
        return (z, y) if j % 2 == 0 else (y, z)

    def place(j, owner, along, xl_=xl):
        z_, y_ = (owner, along) if j % 2 == 0 else (along, owner)
        return z_ * 8 + y_ * 2 + xl_

    core_row = jnp.bitwise_xor(row, 1)
    far_row = ring(row, 2)

    def remote(src, dst, send, recv, row_, col_):
        return pltpu.make_async_remote_copy(
            src_ref=src, dst_ref=dst, send_sem=send, recv_sem=recv, device_id=(row_, col_), device_id_type=MESH
        )

    def cross():
        return remote(t_ref, t_other, xs.at[0], xr.at[0], row, jnp.bitwise_xor(col, 1))

    def t1(j, e, shift, sending):
        owner, along = axes(j)
        to = ring(owner, shift)
        source = owner if sending else ring(owner, -shift)
        src = t_mine.at[e, to * PER_OWNER + j]
        dst = t_all.at[0, j, pl.ds(pl.multiple_of((jnp.bitwise_xor(xl, e) * RING + source) * pairs, pairs), pairs), :]
        n = e * RING + shift
        if shift == 0:
            return pltpu.make_async_copy(src, dst, t1r.at[j, n])
        return remote(src, dst, t1s.at[j, n], t1r.at[j, n], row, place(j, to, along))

    def half(e):
        return pl.ds(pl.multiple_of(jnp.bitwise_xor(xl, e) * (block // 2), block // 2), block // 2)

    def v1(j, shift, sending):
        owner, along = axes(j)
        to = ring(owner, shift)
        source = owner if sending else ring(owner, -shift)
        src = v_mine.at[j, pl.ds(pl.multiple_of(to * SLOTS, SLOTS), SLOTS), :]
        dst = v_all.at[
            j, pl.ds(pl.multiple_of(source * SLOTS, SLOTS), SLOTS), pl.ds(pl.multiple_of(row * width, width), width)
        ]
        if shift == 0:
            return pltpu.make_async_copy(src, dst, v1r.at[j, 0])
        return remote(src, dst, v1s.at[j, shift], v1r.at[j, shift], row, place(j, to, along))

    def v2(j, kind, sending):
        if kind == 0:
            of = row if sending else core_row
        elif kind == 1:
            of = row if sending else far_row
        else:
            of = far_row if sending else ring(core_row, 2)
        part = v_all.at[j, :, pl.ds(pl.multiple_of(of * width, width), width)]
        return remote(part, part, v2s.at[j, kind], v2r.at[j, kind], far_row if kind == 1 else core_row, col)

    def t2(j, kind):
        owner, along = axes(j)
        e = kind % 2
        up = kind in (0, 1, 4)
        from_slot, to_slot = ((0, 1) if up else (0, 2)) if kind < 4 else ((1, 3) if up else (2, 3))
        src, dst = t_all.at[from_slot, j, half(e), :], t_all.at[to_slot, j, half(e), :]
        return remote(
            src, dst, t2s.at[j, kind], t2r.at[j, kind], row, place(j, owner, ring(along, 1 if up else -1))
        )

    def back(j, s, shift, sending):
        owner, along = axes(j)
        to = ring(owner, shift)
        source = owner if sending else ring(owner, -shift)
        src = r_mine.at[s, j, pl.ds(pl.multiple_of(to * SLOTS, SLOTS), SLOTS), :]
        dst = r_all.at[
            j % 2,
            pl.ds(pl.multiple_of((source * 2 + j // 2) * SLOTS, SLOTS), SLOTS),
            pl.ds(pl.multiple_of(ring(along, SHIFT[s]) * block, block), block),
        ]
        n = s * RING + shift
        if shift == 0:
            return pltpu.make_async_copy(src, dst, rr.at[j, n])
        return remote(src, dst, rs.at[j, n], rr.at[j, n], row, place(j, to, along))

    barrier = pltpu.get_barrier_semaphore()
    peers = [(row, place(j, ring(axes(j)[0], shift), axes(j)[1])) for j in (0, 1) for shift in (1, 3, 2)]
    peers += [(row, jnp.bitwise_xor(col, 1)), (core_row, col), (far_row, col)]
    for peer in peers:
        pl.semaphore_signal(barrier, inc=1, device_id=peer, device_id_type=MESH)

    def sort(from_ref):
        for c in range(c_tot):
            stacked[pl.ds(c * pairs, pairs), :] = from_ref[:, pl.ds(c * nvir, nvir)]
        for pair in range(CLASSES // 2):
            column = lax.broadcasted_iota(jnp.int32, (nvir, 2 * LANES), 1) + pair * 2 * LANES
            got = nn_dot(stacked[...], one_hot(code_col[...] == column))
            by_class[2 * pair] = got[:, :LANES]
            by_class[2 * pair + 1] = got[:, LANES:]

    classes = [code_s[c] >> 7 for c in range(c_tot)]

    def arrange(j, e):
        for z_ in range(RING):
            h = z_ * PER_OWNER + j
            for quad in range(c_tot // 4):
                pieces = [
                    by_class[jnp.bitwise_xor(classes[c], h), pl.ds(c * pairs, pairs), :]
                    for c in range(4 * quad, 4 * quad + 4)
                ]
                for part, value in enumerate(pack_quad(pieces)):
                    t_mine[e, h, :, pl.ds(quad * 384 + part * LANES, LANES)] = value.astype(jnp.bfloat16)

    def label(code, lead):
        irrep = jnp.bitwise_xor((code >> 7) & 7, (lead >> 7) & 7)
        return irrep + 8 * ((code >> 10) + (lead >> 10))

    cd_labels = [label(code_row[...], code_s[row * c_here + c]) for c in range(c_here)]
    own = code_s[col]

    def spot(code):
        return jnp.bitwise_xor(code >> 7, own >> 7) * SLOTS + (code & 127)

    spot_row = spot(code_row[...])

    def compress(n):
        load(n).wait()
        ab_label = label(code_col[pl.ds(n * rows, rows), :], own)
        pieces = []
        for c in range(c_here):
            part = v_raw[n, :, pl.ds(c * nvir, nvir)]
            masked = jnp.where(ab_label == cd_labels[c], part, jnp.zeros_like(part))
            pieces.append(nn_dot(masked, picked[...]))
        for part, value in enumerate(pack_quad(pieces)):
            packed[pl.ds(n * rows, rows), pl.ds(part * LANES, LANES)] = value.astype(jnp.bfloat16)

    def permute(j):
        line = lax.broadcasted_iota(jnp.int32, (RING * SLOTS, nvir), 0)
        over = sum((line >= z_ * SLOTS).astype(jnp.int32) for z_ in range(1, RING))
        index = line + over * ((PER_OWNER - 1) * SLOTS) + j * SLOTS
        v_mine[j] = nn_dot(one_hot(spot_row == index), packed[...]).astype(jnp.bfloat16)

    def build_unsort(parity):
        h = jnp.bitwise_xor(code_row[...] >> 7, own >> 7)
        line = ((h >> 2) * 2 + ((h >> 1) & 1)) * SLOTS + (code_row[...] & 127)
        line = jnp.where((h & 1) == parity, line, -1)
        index = lax.broadcasted_iota(jnp.int32, unsort.shape[1:], 0)
        unsort[parity] = one_hot(line == index)

    def arrived(copy):
        if copy.is_remote:
            copy.wait_recv()
        else:
            copy.wait()

    def send_amplitudes(j, e):
        arrange(j, e)
        for shift in ORDER:
            t1(j, e, shift, True).start()

    def send_integrals(j):
        permute(j)
        for shift in ORDER:
            v1(j, shift, True).start()

    def begin_ring(j):
        for shift in ORDER:
            arrived(t1(j, 0, shift, False))
        t2(j, 0).start()
        t2(j, 2).start()

    def join_ring(j):
        for shift in ORDER:
            arrived(t1(j, 1, shift, False))
        t2(j, 1).start()
        t2(j, 3).start()

    def pass_on(j):
        arrived(t2(j, 0))
        t2(j, 4).start()
        arrived(t2(j, 3))
        t2(j, 5).start()

    def over_rows(j):
        for shift in ORDER:
            arrived(v1(j, shift, False))
        v2(j, 0, True).start()
        v2(j, 1, True).start()

    def last_row(j):
        arrived(v2(j, 1, False))
        v2(j, 2, True).start()

    def multiply(j, s):
        r_mine[s, j] = nt_dot(v_all[j], t_all[s, j]).astype(jnp.bfloat16)
        for shift in ORDER:
            back(j, s, shift, True).start()

    def near(j):
        arrived(v2(j, 0, False))
        arrived(v2(j, 2, False))
        multiply(j, 0)
        arrived(t2(j, 1))
        multiply(j, 1)
        arrived(t2(j, 2))
        multiply(j, 2)

    def far(j):
        arrived(t2(j, 4))
        arrived(t2(j, 5))
        multiply(j, 3)

    def finish(parity, s):
        for j in (parity, parity + 2):
            for shift in range(RING):
                arrived(back(j, s, shift, False))
        along = ring(axes(parity)[1], SHIFT[s])
        lanes = pl.ds(pl.multiple_of(along * block, block), block)
        got = tn_dot(r_all[parity, :, lanes], unsort[parity]).astype(jnp.bfloat16)
        for n in range(8):
            xl_, other = n // RING, n % RING
            z_, y_ = (other, along) if parity == 0 else (along, other)
            at = pl.ds(pl.multiple_of(z_ * block + (y_ * 2 + xl_) * pairs, pairs), pairs)
            piece = got[n * pairs : (n + 1) * pairs]
            out_ref[at, :] = piece if parity == 0 else out_ref[at, :] + piece

    sort(t_ref)
    pl.semaphore_wait(barrier, len(peers))
    cross().start()
    send_amplitudes(0, 0)
    send_amplitudes(1, 0)
    send_amplitudes(2, 0)
    send_amplitudes(3, 0)
    picked[...] = one_hot((code_col[...] & 127) == lax.broadcasted_iota(jnp.int32, (nvir, LANES), 1))
    compress(0)
    compress(1)
    compress(2)
    compress(3)
    begin_ring(0)
    compress(4)
    compress(5)
    begin_ring(1)
    compress(6)
    compress(7)
    send_integrals(0)
    begin_ring(2)
    send_integrals(1)
    begin_ring(3)
    arrived(cross())
    sort(t_other)
    send_amplitudes(0, 1)
    send_amplitudes(1, 1)
    send_integrals(2)
    over_rows(0)
    send_amplitudes(2, 1)
    send_amplitudes(3, 1)
    send_integrals(3)
    join_ring(0)
    over_rows(1)
    join_ring(1)
    pass_on(0)
    join_ring(2)
    pass_on(1)
    last_row(0)
    over_rows(2)
    join_ring(3)
    last_row(1)
    over_rows(3)
    build_unsort(0)
    near(0)
    pass_on(2)
    last_row(2)
    near(1)
    far(0)
    pass_on(3)
    last_row(3)
    build_unsort(1)
    far(1)
    near(2)
    near(3)
    far(2)
    finish(0, 0)
    far(3)
    finish(0, 1)
    finish(0, 2)
    finish(0, 3)
    finish(1, 0)
    finish(1, 1)
    finish(1, 2)
    finish(1, 3)

    cross().wait_send()
    for j in range(PER_OWNER):
        for shift in range(1, RING):
            t1(j, 0, shift, True).wait_send()
            t1(j, 1, shift, True).wait_send()
            v1(j, shift, True).wait_send()
        for kind in range(3):
            v2(j, kind, True).wait_send()
        for kind in range(6):
            t2(j, kind).wait_send()
        for s in range(4):
            for shift in range(1, RING):
                back(j, s, shift, True).wait_send()


def blocked(code, amplitudes, integrals, orbital_irrep, orbital_spin):
    nvir = orbital_irrep.shape[0]
    pairs, cd = amplitudes.shape
    ab, cd_here = integrals.shape
    depth = (cd // nvir) * SLOTS
    width = (cd_here // nvir) * SLOTS
    block = 8 * pairs
    tall = RING * SLOTS
    rows = 128
    vmem = pl.BlockSpec(memory_space=pltpu.VMEM)
    dma = pltpu.SemaphoreType.DMA
    bf16 = jnp.bfloat16
    return pl.pallas_call(
        contract,
        out_shape=jax.ShapeDtypeStruct((RING * block, nvir), bf16),
        in_specs=[pl.BlockSpec(memory_space=pltpu.SMEM), vmem, vmem, vmem, pl.BlockSpec(memory_space=pl.ANY)],
        out_specs=vmem,
        scratch_shapes=[
            pltpu.VMEM((ab // rows, rows, cd_here), bf16),
            pltpu.VMEM((pairs, cd), bf16),
            pltpu.VMEM((cd // nvir * pairs, nvir), bf16),
            pltpu.VMEM((CLASSES, cd // nvir * pairs, LANES), jnp.float32),
            pltpu.VMEM((2, CLASSES, pairs, depth), bf16),
            pltpu.VMEM((nvir, LANES), bf16),
            pltpu.VMEM((ab, width), bf16),
            pltpu.VMEM((PER_OWNER, tall, width), bf16),
            pltpu.VMEM((2, CLASSES // 2 * SLOTS, nvir), bf16),
            pltpu.VMEM((RING, PER_OWNER, block, depth), bf16),
            pltpu.VMEM((PER_OWNER, tall, depth), bf16),
            pltpu.VMEM((RING, PER_OWNER, tall, block), bf16),
            pltpu.VMEM((2, CLASSES // 2 * SLOTS, RING * block), bf16),
            dma((ab // rows,)),
            *[dma((PER_OWNER, 8))] * 2,
            *[dma((1,))] * 2,
            *[dma((PER_OWNER, 4))] * 2,
            *[dma((PER_OWNER, 3))] * 2,
            *[dma((PER_OWNER, 6))] * 2,
            *[dma((PER_OWNER, 16))] * 2,
        ],
        compiler_params=pltpu.CompilerParams(
            collective_id=0, has_side_effects=True, vmem_limit_bytes=38 * MIB
        ),
        name="contract",
    )(code, code[:, None], code[None, :], amplitudes, integrals)


def local(amplitudes, integrals, orbital_irrep, orbital_spin):
    count = jnp.arange(orbital_irrep.shape[0], dtype=jnp.int32)
    same = (orbital_irrep[:, None] == orbital_irrep[None, :]) & (orbital_spin[:, None] == orbital_spin[None, :])
    rank = jnp.sum((same & (count[None, :] < count[:, None])).astype(jnp.int32), axis=1)
    return lax.cond(
        jnp.max(rank) < SLOTS,
        blocked,
        lambda code, *args: dense(*args),
        (orbital_irrep + 8 * orbital_spin) * LANES + rank,
        amplitudes,
        integrals,
        orbital_irrep,
        orbital_spin,
    )


def solution(mesh):
    placed = (P(("row", "col"), None), P("col", "row"), P(), P())
    return jax.shard_map(
        local, mesh=mesh, in_specs=placed, out_specs=P("row", "col"), check_vma=False
    )
```

```python
import functools

import jax
import jax.numpy as jnp
from jax import lax
from jax.experimental import pallas as pl
from jax.experimental.pallas import tpu as pltpu
from jax.sharding import PartitionSpec as P

MESH = pl.DeviceIdType.MESH
CLASSES = 16
SLOTS = 96
RING = 4
PER_OWNER = CLASSES // RING
ORDER = (1, 3, 2, 0)
SHIFT = (0, -1, 1, 2)
LANES = 128
MIB = 1 << 20


def nt_dot(lhs, rhs):
    return lax.dot_general(lhs, rhs, (((1,), (1,)), ((), ())), preferred_element_type=jnp.float32)


def nn_dot(lhs, rhs):
    return jnp.dot(lhs, rhs, preferred_element_type=jnp.float32)


def tn_dot(lhs, rhs):
    return lax.dot_general(lhs, rhs, (((0,), (0,)), ((), ())), preferred_element_type=jnp.float32)


def pair_labels(first, count, orbital_irrep, orbital_spin):
    lead_irrep = lax.dynamic_slice_in_dim(orbital_irrep, first, count, 0)
    lead_spin = lax.dynamic_slice_in_dim(orbital_spin, first, count, 0)
    labels = jnp.bitwise_xor(lead_irrep[:, None], orbital_irrep[None, :]) + 8 * (
        lead_spin[:, None] + orbital_spin[None, :]
    )
    return labels.reshape(-1)


def dense(amplitudes, integrals, orbital_irrep, orbital_spin):
    virtuals = orbital_irrep.shape[0]
    a_count = integrals.shape[0] // virtuals
    c_count = integrals.shape[1] // virtuals
    ab_labels = pair_labels(lax.axis_index("col") * a_count, a_count, orbital_irrep, orbital_spin)
    cd_labels = pair_labels(lax.axis_index("row") * c_count, c_count, orbital_irrep, orbital_spin)
    masked = jnp.where(
        ab_labels[:, None] == cd_labels[None, :], integrals, jnp.zeros((), integrals.dtype)
    )
    grid_rows = lax.all_gather(amplitudes, "col", axis=0, tiled=True)
    regrouped = lax.all_to_all(grid_rows, "row", split_axis=1, concat_axis=0, tiled=True)
    partial_sums = nt_dot(regrouped, masked)
    return lax.psum_scatter(partial_sums, "row", scatter_dimension=0, tiled=True).astype(
        jnp.bfloat16
    )


def one_hot(hit):
    return jnp.where(hit, 1.0, 0.0).astype(jnp.bfloat16)


def pack_quad(pieces):
    first, second, third, fourth = pieces
    lane = lax.broadcasted_iota(jnp.int32, first.shape, 1)
    zero = jnp.zeros_like(first)
    second = pltpu.roll(second, 96, 1)
    third = pltpu.roll(third, 64, 1)
    fourth = pltpu.roll(fourth, 32, 1)
    return (
        first + jnp.where(lane >= 96, second, zero),
        jnp.where(lane < 64, second, zero) + jnp.where(lane >= 64, third, zero),
        jnp.where(lane < 32, third, zero) + fourth,
    )


def contract(
    code_s, code_col, code_row, t_ref, v_hbm, out_ref,
    v_raw, t_other, stacked, by_class, t_mine, picked, packed, v_mine, unsort, t_all, v_all, r_mine, r_all,
    loads, t1s, t1r, xs, xr, v1s, v1r, v2s, v2r, t2s, t2r, rs, rr,
):
    row, col = lax.axis_index("row"), lax.axis_index("col")
    z, y, xl = col // 8, (col // 2) % 4, col % 2
    nvir = code_col.shape[0]
    pairs, c_tot = t_ref.shape[0], t_ref.shape[1] // nvir
    c_here = v_hbm.shape[1] // nvir
    block = 8 * pairs
    width = c_here * SLOTS
    chunks, rows = v_raw.shape[0], v_raw.shape[1]

    def load(n):
        return pltpu.make_async_copy(v_hbm.at[pl.ds(n * rows, rows), :], v_raw.at[n], loads.at[n])

    for n in range(chunks):
        load(n).start()

    def ring(value, shift):
        return lax.rem(value + (shift + RING), RING)

    def axes(j):
        return (z, y) if j % 2 == 0 else (y, z)

    def place(j, owner, along, xl_=xl):
        z_, y_ = (owner, along) if j % 2 == 0 else (along, owner)
        return z_ * 8 + y_ * 2 + xl_

    core_row = jnp.bitwise_xor(row, 1)
    far_row = ring(row, 2)

    def remote(src, dst, send, recv, row_, col_):
        return pltpu.make_async_remote_copy(
            src_ref=src, dst_ref=dst, send_sem=send, recv_sem=recv, device_id=(row_, col_), device_id_type=MESH
        )

    def cross():
        return remote(t_ref, t_other, xs.at[0], xr.at[0], row, jnp.bitwise_xor(col, 1))

    def t1(j, e, shift, sending):
        owner, along = axes(j)
        to = ring(owner, shift)
        source = owner if sending else ring(owner, -shift)
        src = t_mine.at[e, to * PER_OWNER + j]
        dst = t_all.at[0, j, pl.ds(pl.multiple_of((jnp.bitwise_xor(xl, e) * RING + source) * pairs, pairs), pairs), :]
        n = e * RING + shift
        if shift == 0:
            return pltpu.make_async_copy(src, dst, t1r.at[j, n])
        return remote(src, dst, t1s.at[j, n], t1r.at[j, n], row, place(j, to, along))

    def half(e):
        return pl.ds(pl.multiple_of(jnp.bitwise_xor(xl, e) * (block // 2), block // 2), block // 2)

    def v1(j, shift, sending):
        owner, along = axes(j)
        to = ring(owner, shift)
        source = owner if sending else ring(owner, -shift)
        src = v_mine.at[j, pl.ds(pl.multiple_of(to * SLOTS, SLOTS), SLOTS), :]
        dst = v_all.at[
            j, pl.ds(pl.multiple_of(source * SLOTS, SLOTS), SLOTS), pl.ds(pl.multiple_of(row * width, width), width)
        ]
        if shift == 0:
            return pltpu.make_async_copy(src, dst, v1r.at[j, 0])
        return remote(src, dst, v1s.at[j, shift], v1r.at[j, shift], row, place(j, to, along))

    def v2(j, kind, sending):
        if kind == 0:
            of = row if sending else core_row
        elif kind == 1:
            of = row if sending else far_row
        else:
            of = far_row if sending else ring(core_row, 2)
        part = v_all.at[j, :, pl.ds(pl.multiple_of(of * width, width), width)]
        return remote(part, part, v2s.at[j, kind], v2r.at[j, kind], far_row if kind == 1 else core_row, col)

    def t2(j, kind):
        owner, along = axes(j)
        e = kind % 2
        up = kind in (0, 1, 4)
        from_slot, to_slot = ((0, 1) if up else (0, 2)) if kind < 4 else ((1, 3) if up else (2, 3))
        src, dst = t_all.at[from_slot, j, half(e), :], t_all.at[to_slot, j, half(e), :]
        return remote(
            src, dst, t2s.at[j, kind], t2r.at[j, kind], row, place(j, owner, ring(along, 1 if up else -1))
        )

    def back(j, s, shift, sending):
        owner, along = axes(j)
        to = ring(owner, shift)
        source = owner if sending else ring(owner, -shift)
        src = r_mine.at[s, j, pl.ds(pl.multiple_of(to * SLOTS, SLOTS), SLOTS), :]
        dst = r_all.at[
            j % 2,
            pl.ds(pl.multiple_of((source * 2 + j // 2) * SLOTS, SLOTS), SLOTS),
            pl.ds(pl.multiple_of(ring(along, SHIFT[s]) * block, block), block),
        ]
        n = s * RING + shift
        if shift == 0:
            return pltpu.make_async_copy(src, dst, rr.at[j, n])
        return remote(src, dst, rs.at[j, n], rr.at[j, n], row, place(j, to, along))

    barrier = pltpu.get_barrier_semaphore()
    peers = [(row, place(j, ring(axes(j)[0], shift), axes(j)[1])) for j in (0, 1) for shift in (1, 3, 2)]
    peers += [(row, jnp.bitwise_xor(col, 1)), (core_row, col), (far_row, col)]
    for peer in peers:
        pl.semaphore_signal(barrier, inc=1, device_id=peer, device_id_type=MESH)

    def sort(from_ref):
        for c in range(c_tot):
            stacked[pl.ds(c * pairs, pairs), :] = from_ref[:, pl.ds(c * nvir, nvir)]
        for pair in range(CLASSES // 2):
            column = lax.broadcasted_iota(jnp.int32, (nvir, 2 * LANES), 1) + pair * 2 * LANES
            got = nn_dot(stacked[...], one_hot(code_col[...] == column))
            by_class[2 * pair] = got[:, :LANES]
            by_class[2 * pair + 1] = got[:, LANES:]

    classes = [code_s[c] >> 7 for c in range(c_tot)]

    def arrange(j, e):
        for z_ in range(RING):
            h = z_ * PER_OWNER + j
            for quad in range(c_tot // 4):
                pieces = [
                    by_class[jnp.bitwise_xor(classes[c], h), pl.ds(c * pairs, pairs), :]
                    for c in range(4 * quad, 4 * quad + 4)
                ]
                for part, value in enumerate(pack_quad(pieces)):
                    t_mine[e, h, :, pl.ds(quad * 384 + part * LANES, LANES)] = value.astype(jnp.bfloat16)

    def label(code, lead):
        irrep = jnp.bitwise_xor((code >> 7) & 7, (lead >> 7) & 7)
        return irrep + 8 * ((code >> 10) + (lead >> 10))

    cd_labels = [label(code_row[...], code_s[row * c_here + c]) for c in range(c_here)]
    own = code_s[col]

    def spot(code):
        return jnp.bitwise_xor(code >> 7, own >> 7) * SLOTS + (code & 127)

    spot_row = spot(code_row[...])

    def compress(n):
        load(n).wait()
        ab_label = label(code_col[pl.ds(n * rows, rows), :], own)
        pieces = []
        for c in range(c_here):
            part = v_raw[n, :, pl.ds(c * nvir, nvir)]
            masked = jnp.where(ab_label == cd_labels[c], part, jnp.zeros_like(part))
            pieces.append(nn_dot(masked, picked[...]))
        for part, value in enumerate(pack_quad(pieces)):
            packed[pl.ds(n * rows, rows), pl.ds(part * LANES, LANES)] = value.astype(jnp.bfloat16)

    def permute(j):
        line = lax.broadcasted_iota(jnp.int32, (RING * SLOTS, nvir), 0)
        over = sum((line >= z_ * SLOTS).astype(jnp.int32) for z_ in range(1, RING))
        index = line + over * ((PER_OWNER - 1) * SLOTS) + j * SLOTS
        v_mine[j] = nn_dot(one_hot(spot_row == index), packed[...]).astype(jnp.bfloat16)

    def build_unsort(parity):
        h = jnp.bitwise_xor(code_row[...] >> 7, own >> 7)
        line = ((h >> 2) * 2 + ((h >> 1) & 1)) * SLOTS + (code_row[...] & 127)
        line = jnp.where((h & 1) == parity, line, -1)
        index = lax.broadcasted_iota(jnp.int32, unsort.shape[1:], 0)
        unsort[parity] = one_hot(line == index)

    def arrived(copy):
        if copy.is_remote:
            copy.wait_recv()
        else:
            copy.wait()

    def send_amplitudes(j, e):
        arrange(j, e)
        for shift in ORDER:
            t1(j, e, shift, True).start()

    def send_integrals(j):
        permute(j)
        for shift in ORDER:
            v1(j, shift, True).start()

    def begin_ring(j):
        for shift in ORDER:
            arrived(t1(j, 0, shift, False))
        t2(j, 0).start()
        t2(j, 2).start()

    def join_ring(j):
        for shift in ORDER:
            arrived(t1(j, 1, shift, False))
        t2(j, 1).start()
        t2(j, 3).start()

    def pass_on(j):
        arrived(t2(j, 0))
        t2(j, 4).start()
        arrived(t2(j, 3))
        t2(j, 5).start()

    def over_rows(j):
        for shift in ORDER:
            arrived(v1(j, shift, False))
        v2(j, 0, True).start()
        v2(j, 1, True).start()

    def last_row(j):
        arrived(v2(j, 1, False))
        v2(j, 2, True).start()

    def multiply(j, s):
        r_mine[s, j] = nt_dot(v_all[j], t_all[s, j]).astype(jnp.bfloat16)
        for shift in (2, 1, 3, 0):
            back(j, s, shift, True).start()

    def near(j):
        arrived(v2(j, 0, False))
        arrived(v2(j, 2, False))
        multiply(j, 0)
        arrived(t2(j, 1))
        multiply(j, 1)
        arrived(t2(j, 2))
        multiply(j, 2)

    def far(j):
        arrived(t2(j, 4))
        arrived(t2(j, 5))
        multiply(j, 3)

    def finish(parity, s):
        for j in (parity, parity + 2):
            for shift in range(RING):
                arrived(back(j, s, shift, False))
        along = ring(axes(parity)[1], SHIFT[s])
        lanes = pl.ds(pl.multiple_of(along * block, block), block)
        got = tn_dot(r_all[parity, :, lanes], unsort[parity]).astype(jnp.bfloat16)
        for n in range(8):
            xl_, other = n // RING, n % RING
            z_, y_ = (other, along) if parity == 0 else (along, other)
            at = pl.ds(pl.multiple_of(z_ * block + (y_ * 2 + xl_) * pairs, pairs), pairs)
            piece = got[n * pairs : (n + 1) * pairs]
            out_ref[at, :] = piece if parity == 0 else out_ref[at, :] + piece

    sort(t_ref)
    pl.semaphore_wait(barrier, len(peers))
    cross().start()
    send_amplitudes(0, 0)
    send_amplitudes(1, 0)
    send_amplitudes(2, 0)
    send_amplitudes(3, 0)
    picked[...] = one_hot((code_col[...] & 127) == lax.broadcasted_iota(jnp.int32, (nvir, LANES), 1))
    compress(0)
    compress(1)
    compress(2)
    compress(3)
    begin_ring(0)
    compress(4)
    compress(5)
    begin_ring(1)
    compress(6)
    compress(7)
    send_integrals(0)
    begin_ring(2)
    send_integrals(1)
    begin_ring(3)
    arrived(cross())
    sort(t_other)
    send_amplitudes(0, 1)
    send_amplitudes(1, 1)
    send_integrals(2)
    over_rows(0)
    send_amplitudes(2, 1)
    send_amplitudes(3, 1)
    send_integrals(3)
    join_ring(0)
    over_rows(1)
    join_ring(1)
    pass_on(0)
    join_ring(2)
    pass_on(1)
    last_row(0)
    over_rows(2)
    join_ring(3)
    last_row(1)
    over_rows(3)
    build_unsort(0)
    near(0)
    pass_on(2)
    last_row(2)
    near(1)
    far(0)
    pass_on(3)
    last_row(3)
    build_unsort(1)
    far(1)
    near(2)
    near(3)
    far(2)
    finish(0, 0)
    far(3)
    finish(0, 1)
    finish(0, 2)
    finish(0, 3)
    finish(1, 0)
    finish(1, 1)
    finish(1, 2)
    finish(1, 3)

    cross().wait_send()
    for j in range(PER_OWNER):
        for shift in range(1, RING):
            t1(j, 0, shift, True).wait_send()
            t1(j, 1, shift, True).wait_send()
            v1(j, shift, True).wait_send()
        for kind in range(3):
            v2(j, kind, True).wait_send()
        for kind in range(6):
            t2(j, kind).wait_send()
        for s in range(4):
            for shift in range(1, RING):
                back(j, s, shift, True).wait_send()


def blocked(code, amplitudes, integrals, orbital_irrep, orbital_spin):
    nvir = orbital_irrep.shape[0]
    pairs, cd = amplitudes.shape
    ab, cd_here = integrals.shape
    depth = (cd // nvir) * SLOTS
    width = (cd_here // nvir) * SLOTS
    block = 8 * pairs
    tall = RING * SLOTS
    rows = 128
    vmem = pl.BlockSpec(memory_space=pltpu.VMEM)
    dma = pltpu.SemaphoreType.DMA
    bf16 = jnp.bfloat16
    return pl.pallas_call(
        contract,
        out_shape=jax.ShapeDtypeStruct((RING * block, nvir), bf16),
        in_specs=[pl.BlockSpec(memory_space=pltpu.SMEM), vmem, vmem, vmem, pl.BlockSpec(memory_space=pl.ANY)],
        out_specs=vmem,
        scratch_shapes=[
            pltpu.VMEM((ab // rows, rows, cd_here), bf16),
            pltpu.VMEM((pairs, cd), bf16),
            pltpu.VMEM((cd // nvir * pairs, nvir), bf16),
            pltpu.VMEM((CLASSES, cd // nvir * pairs, LANES), jnp.float32),
            pltpu.VMEM((2, CLASSES, pairs, depth), bf16),
            pltpu.VMEM((nvir, LANES), bf16),
            pltpu.VMEM((ab, width), bf16),
            pltpu.VMEM((PER_OWNER, tall, width), bf16),
            pltpu.VMEM((2, CLASSES // 2 * SLOTS, nvir), bf16),
            pltpu.VMEM((RING, PER_OWNER, block, depth), bf16),
            pltpu.VMEM((PER_OWNER, tall, depth), bf16),
            pltpu.VMEM((RING, PER_OWNER, tall, block), bf16),
            pltpu.VMEM((2, CLASSES // 2 * SLOTS, RING * block), bf16),
            dma((ab // rows,)),
            *[dma((PER_OWNER, 8))] * 2,
            *[dma((1,))] * 2,
            *[dma((PER_OWNER, 4))] * 2,
            *[dma((PER_OWNER, 3))] * 2,
            *[dma((PER_OWNER, 6))] * 2,
            *[dma((PER_OWNER, 16))] * 2,
        ],
        compiler_params=pltpu.CompilerParams(
            collective_id=0, has_side_effects=True, vmem_limit_bytes=38 * MIB
        ),
        name="contract",
    )(code, code[:, None], code[None, :], amplitudes, integrals)


def local(amplitudes, integrals, orbital_irrep, orbital_spin):
    group = orbital_irrep + 8 * orbital_spin
    count = jnp.arange(group.shape[0], dtype=jnp.int32)
    earlier = (group[:, None] == group[None, :]) & (count[None, :] < count[:, None])
    rank = jnp.sum(earlier.astype(jnp.int32), axis=1)
    return lax.cond(
        jnp.max(rank) < SLOTS,
        blocked,
        lambda code, *args: dense(*args),
        group * LANES + rank,
        amplitudes,
        integrals,
        orbital_irrep,
        orbital_spin,
    )


def solution(mesh):
    placed = (P(("row", "col"), None), P("col", "row"), P(), P())
    return jax.shard_map(
        local, mesh=mesh, in_specs=placed, out_specs=P("row", "col"), check_vma=False
    )
```

```python
import functools

import jax
import jax.numpy as jnp
from jax import lax
from jax.experimental import pallas as pl
from jax.experimental.pallas import tpu as pltpu
from jax.sharding import PartitionSpec as P

MESH = pl.DeviceIdType.MESH
CLASSES = 16
SLOTS = 96
RING = 4
PER_OWNER = CLASSES // RING
ORDER = (1, 3, 2, 0)
SHIFT = (0, -1, 1, 2)
LANES = 128
MIB = 1 << 20


def nt_dot(lhs, rhs):
    return lax.dot_general(lhs, rhs, (((1,), (1,)), ((), ())), preferred_element_type=jnp.float32)


def nn_dot(lhs, rhs):
    return jnp.dot(lhs, rhs, preferred_element_type=jnp.float32)


def tn_dot(lhs, rhs):
    return lax.dot_general(lhs, rhs, (((0,), (0,)), ((), ())), preferred_element_type=jnp.float32)


def pair_labels(first, count, orbital_irrep, orbital_spin):
    lead_irrep = lax.dynamic_slice_in_dim(orbital_irrep, first, count, 0)
    lead_spin = lax.dynamic_slice_in_dim(orbital_spin, first, count, 0)
    labels = jnp.bitwise_xor(lead_irrep[:, None], orbital_irrep[None, :]) + 8 * (
        lead_spin[:, None] + orbital_spin[None, :]
    )
    return labels.reshape(-1)


def dense(amplitudes, integrals, orbital_irrep, orbital_spin):
    virtuals = orbital_irrep.shape[0]
    a_count = integrals.shape[0] // virtuals
    c_count = integrals.shape[1] // virtuals
    ab_labels = pair_labels(lax.axis_index("col") * a_count, a_count, orbital_irrep, orbital_spin)
    cd_labels = pair_labels(lax.axis_index("row") * c_count, c_count, orbital_irrep, orbital_spin)
    masked = jnp.where(
        ab_labels[:, None] == cd_labels[None, :], integrals, jnp.zeros((), integrals.dtype)
    )
    grid_rows = lax.all_gather(amplitudes, "col", axis=0, tiled=True)
    regrouped = lax.all_to_all(grid_rows, "row", split_axis=1, concat_axis=0, tiled=True)
    partial_sums = nt_dot(regrouped, masked)
    return lax.psum_scatter(partial_sums, "row", scatter_dimension=0, tiled=True).astype(
        jnp.bfloat16
    )


def one_hot(hit):
    return jnp.where(hit, 1.0, 0.0).astype(jnp.bfloat16)


def pack_quad(pieces):
    first, second, third, fourth = pieces
    lane = lax.broadcasted_iota(jnp.int32, first.shape, 1)
    zero = jnp.zeros_like(first)
    second = pltpu.roll(second, 96, 1)
    third = pltpu.roll(third, 64, 1)
    fourth = pltpu.roll(fourth, 32, 1)
    return (
        first + jnp.where(lane >= 96, second, zero),
        jnp.where(lane < 64, second, zero) + jnp.where(lane >= 64, third, zero),
        jnp.where(lane < 32, third, zero) + fourth,
    )


def contract(
    code_s, code_col, code_row, t_ref, v_hbm, out_ref,
    v_raw, t_other, stacked, by_class, t_mine, picked, packed, v_mine, unsort, t_all, v_all, r_mine, r_all,
    loads, t1s, t1r, xs, xr, v1s, v1r, v2s, v2r, t2s, t2r, rs, rr,
):
    row, col = lax.axis_index("row"), lax.axis_index("col")
    z, y, xl = col // 8, (col // 2) % 4, col % 2
    nvir = code_col.shape[0]
    pairs, c_tot = t_ref.shape[0], t_ref.shape[1] // nvir
    c_here = v_hbm.shape[1] // nvir
    block = 8 * pairs
    width = c_here * SLOTS
    chunks, rows = v_raw.shape[0], v_raw.shape[1]

    def load(n):
        return pltpu.make_async_copy(v_hbm.at[pl.ds(n * rows, rows), :], v_raw.at[n], loads.at[n])

    for n in range(chunks):
        load(n).start()

    def ring(value, shift):
        return lax.rem(value + (shift + RING), RING)

    def axes(j):
        return (z, y) if j % 2 == 0 else (y, z)

    def place(j, owner, along, xl_=xl):
        z_, y_ = (owner, along) if j % 2 == 0 else (along, owner)
        return z_ * 8 + y_ * 2 + xl_

    core_row = jnp.bitwise_xor(row, 1)
    far_row = ring(row, 2)

    def remote(src, dst, send, recv, row_, col_):
        return pltpu.make_async_remote_copy(
            src_ref=src, dst_ref=dst, send_sem=send, recv_sem=recv, device_id=(row_, col_), device_id_type=MESH
        )

    def cross():
        return remote(t_ref, t_other, xs.at[0], xr.at[0], row, jnp.bitwise_xor(col, 1))

    def t1(j, e, shift, sending):
        owner, along = axes(j)
        to = ring(owner, shift)
        source = owner if sending else ring(owner, -shift)
        src = t_mine.at[e, to * PER_OWNER + j]
        dst = t_all.at[0, j, pl.ds(pl.multiple_of((jnp.bitwise_xor(xl, e) * RING + source) * pairs, pairs), pairs), :]
        n = e * RING + shift
        if shift == 0:
            return pltpu.make_async_copy(src, dst, t1r.at[j, n])
        return remote(src, dst, t1s.at[j, n], t1r.at[j, n], row, place(j, to, along))

    def half(e):
        return pl.ds(pl.multiple_of(jnp.bitwise_xor(xl, e) * (block // 2), block // 2), block // 2)

    def v1(j, shift, sending):
        owner, along = axes(j)
        to = ring(owner, shift)
        source = owner if sending else ring(owner, -shift)
        src = v_mine.at[j, pl.ds(pl.multiple_of(to * SLOTS, SLOTS), SLOTS), :]
        dst = v_all.at[
            j, pl.ds(pl.multiple_of(source * SLOTS, SLOTS), SLOTS), pl.ds(pl.multiple_of(row * width, width), width)
        ]
        if shift == 0:
            return pltpu.make_async_copy(src, dst, v1r.at[j, 0])
        return remote(src, dst, v1s.at[j, shift], v1r.at[j, shift], row, place(j, to, along))

    def v2(j, kind, sending):
        if kind == 0:
            of = row if sending else core_row
        elif kind == 1:
            of = row if sending else far_row
        else:
            of = far_row if sending else ring(core_row, 2)
        part = v_all.at[j, :, pl.ds(pl.multiple_of(of * width, width), width)]
        return remote(part, part, v2s.at[j, kind], v2r.at[j, kind], far_row if kind == 1 else core_row, col)

    def t2(j, kind):
        owner, along = axes(j)
        e = kind % 2
        up = kind in (0, 1, 4)
        from_slot, to_slot = ((0, 1) if up else (0, 2)) if kind < 4 else ((1, 3) if up else (2, 3))
        src, dst = t_all.at[from_slot, j, half(e), :], t_all.at[to_slot, j, half(e), :]
        return remote(
            src, dst, t2s.at[j, kind], t2r.at[j, kind], row, place(j, owner, ring(along, 1 if up else -1))
        )

    def back(j, s, shift, sending):
        owner, along = axes(j)
        to = ring(owner, shift)
        source = owner if sending else ring(owner, -shift)
        src = r_mine.at[s, j, pl.ds(pl.multiple_of(to * SLOTS, SLOTS), SLOTS), :]
        dst = r_all.at[
            j % 2,
            ring(along, SHIFT[s]),
            pl.ds(pl.multiple_of((source * 2 + j // 2) * SLOTS, SLOTS), SLOTS),
            :,
        ]
        n = s * RING + shift
        if shift == 0:
            return pltpu.make_async_copy(src, dst, rr.at[j, n])
        return remote(src, dst, rs.at[j, n], rr.at[j, n], row, place(j, to, along))

    barrier = pltpu.get_barrier_semaphore()
    peers = [(row, place(j, ring(axes(j)[0], shift), axes(j)[1])) for j in (0, 1) for shift in (1, 3, 2)]
    peers += [(row, jnp.bitwise_xor(col, 1)), (core_row, col), (far_row, col)]
    for peer in peers:
        pl.semaphore_signal(barrier, inc=1, device_id=peer, device_id_type=MESH)

    def sort(from_ref):
        for c in range(c_tot):
            stacked[pl.ds(c * pairs, pairs), :] = from_ref[:, pl.ds(c * nvir, nvir)]
        for pair in range(CLASSES // 2):
            column = lax.broadcasted_iota(jnp.int32, (nvir, 2 * LANES), 1) + pair * 2 * LANES
            got = nn_dot(stacked[...], one_hot(code_col[...] == column))
            by_class[2 * pair] = got[:, :LANES]
            by_class[2 * pair + 1] = got[:, LANES:]

    classes = [code_s[c] >> 7 for c in range(c_tot)]

    def arrange(j, e):
        for z_ in range(RING):
            h = z_ * PER_OWNER + j
            for quad in range(c_tot // 4):
                pieces = [
                    by_class[jnp.bitwise_xor(classes[c], h), pl.ds(c * pairs, pairs), :]
                    for c in range(4 * quad, 4 * quad + 4)
                ]
                for part, value in enumerate(pack_quad(pieces)):
                    t_mine[e, h, :, pl.ds(quad * 384 + part * LANES, LANES)] = value.astype(jnp.bfloat16)

    def label(code, lead):
        irrep = jnp.bitwise_xor((code >> 7) & 7, (lead >> 7) & 7)
        return irrep + 8 * ((code >> 10) + (lead >> 10))

    cd_labels = [label(code_row[...], code_s[row * c_here + c]) for c in range(c_here)]
    own = code_s[col]

    def spot(code):
        return jnp.bitwise_xor(code >> 7, own >> 7) * SLOTS + (code & 127)

    spot_row = spot(code_row[...])

    def compress(n):
        load(n).wait()
        ab_label = label(code_col[pl.ds(n * rows, rows), :], own)
        pieces = []
        for c in range(c_here):
            part = v_raw[n, :, pl.ds(c * nvir, nvir)]
            masked = jnp.where(ab_label == cd_labels[c], part, jnp.zeros_like(part))
            pieces.append(nn_dot(masked, picked[...]))
        for part, value in enumerate(pack_quad(pieces)):
            packed[pl.ds(n * rows, rows), pl.ds(part * LANES, LANES)] = value.astype(jnp.bfloat16)

    def permute(j):
        line = lax.broadcasted_iota(jnp.int32, (RING * SLOTS, nvir), 0)
        over = sum((line >= z_ * SLOTS).astype(jnp.int32) for z_ in range(1, RING))
        index = line + over * ((PER_OWNER - 1) * SLOTS) + j * SLOTS
        v_mine[j] = nn_dot(one_hot(spot_row == index), packed[...]).astype(jnp.bfloat16)

    def build_unsort(parity):
        h = jnp.bitwise_xor(code_row[...] >> 7, own >> 7)
        line = ((h >> 2) * 2 + ((h >> 1) & 1)) * SLOTS + (code_row[...] & 127)
        line = jnp.where((h & 1) == parity, line, -1)
        index = lax.broadcasted_iota(jnp.int32, unsort.shape[1:], 0)
        unsort[parity] = one_hot(line == index)

    def arrived(copy):
        if copy.is_remote:
            copy.wait_recv()
        else:
            copy.wait()

    def send_amplitudes(j, e):
        arrange(j, e)
        for shift in ORDER:
            t1(j, e, shift, True).start()

    def send_integrals(j):
        permute(j)
        for shift in ORDER:
            v1(j, shift, True).start()

    def begin_ring(j):
        for shift in ORDER:
            arrived(t1(j, 0, shift, False))
        t2(j, 0).start()
        t2(j, 2).start()

    def join_ring(j):
        for shift in ORDER:
            arrived(t1(j, 1, shift, False))
        t2(j, 1).start()
        t2(j, 3).start()

    def pass_on(j):
        arrived(t2(j, 0))
        t2(j, 4).start()
        arrived(t2(j, 3))
        t2(j, 5).start()

    def over_rows(j):
        for shift in ORDER:
            arrived(v1(j, shift, False))
        v2(j, 0, True).start()
        v2(j, 1, True).start()

    def last_row(j):
        arrived(v2(j, 1, False))
        v2(j, 2, True).start()

    def multiply(j, s):
        r_mine[s, j] = nt_dot(v_all[j], t_all[s, j]).astype(jnp.bfloat16)
        for shift in (2, 1, 3, 0):
            back(j, s, shift, True).start()

    def near(j):
        arrived(v2(j, 0, False))
        arrived(v2(j, 2, False))
        multiply(j, 0)
        arrived(t2(j, 1))
        multiply(j, 1)
        arrived(t2(j, 2))
        multiply(j, 2)

    def far(j):
        arrived(t2(j, 4))
        arrived(t2(j, 5))
        multiply(j, 3)

    def finish(parity, s):
        for j in (parity, parity + 2):
            for shift in range(RING):
                arrived(back(j, s, shift, False))
        along = ring(axes(parity)[1], SHIFT[s])
        got = tn_dot(r_all[parity, along], unsort[parity]).astype(jnp.bfloat16)
        for n in range(8):
            xl_, other = n // RING, n % RING
            z_, y_ = (other, along) if parity == 0 else (along, other)
            at = pl.ds(pl.multiple_of(z_ * block + (y_ * 2 + xl_) * pairs, pairs), pairs)
            piece = got[n * pairs : (n + 1) * pairs]
            out_ref[at, :] = piece if parity == 0 else out_ref[at, :] + piece

    sort(t_ref)
    pl.semaphore_wait(barrier, len(peers))
    cross().start()
    send_amplitudes(0, 0)
    send_amplitudes(1, 0)
    send_amplitudes(2, 0)
    send_amplitudes(3, 0)
    picked[...] = one_hot((code_col[...] & 127) == lax.broadcasted_iota(jnp.int32, (nvir, LANES), 1))
    compress(0)
    compress(1)
    compress(2)
    compress(3)
    begin_ring(0)
    compress(4)
    compress(5)
    begin_ring(1)
    compress(6)
    compress(7)
    send_integrals(0)
    begin_ring(2)
    send_integrals(1)
    begin_ring(3)
    arrived(cross())
    sort(t_other)
    send_amplitudes(0, 1)
    send_amplitudes(1, 1)
    send_integrals(2)
    over_rows(0)
    send_amplitudes(2, 1)
    send_amplitudes(3, 1)
    send_integrals(3)
    join_ring(0)
    over_rows(1)
    join_ring(1)
    pass_on(0)
    join_ring(2)
    pass_on(1)
    last_row(0)
    over_rows(2)
    join_ring(3)
    last_row(1)
    over_rows(3)
    build_unsort(0)
    near(0)
    pass_on(2)
    last_row(2)
    near(1)
    far(0)
    pass_on(3)
    last_row(3)
    build_unsort(1)
    far(1)
    near(2)
    far(2)
    near(3)
    far(3)
    finish(0, 0)
    finish(0, 1)
    finish(0, 2)
    finish(0, 3)
    finish(1, 0)
    finish(1, 1)
    finish(1, 2)
    finish(1, 3)

    cross().wait_send()
    for j in range(PER_OWNER):
        for shift in range(1, RING):
            t1(j, 0, shift, True).wait_send()
            t1(j, 1, shift, True).wait_send()
            v1(j, shift, True).wait_send()
        for kind in range(3):
            v2(j, kind, True).wait_send()
        for kind in range(6):
            t2(j, kind).wait_send()
        for s in range(4):
            for shift in range(1, RING):
                back(j, s, shift, True).wait_send()


def blocked(code, amplitudes, integrals, orbital_irrep, orbital_spin):
    nvir = orbital_irrep.shape[0]
    pairs, cd = amplitudes.shape
    ab, cd_here = integrals.shape
    depth = (cd // nvir) * SLOTS
    width = (cd_here // nvir) * SLOTS
    block = 8 * pairs
    tall = RING * SLOTS
    rows = 128
    vmem = pl.BlockSpec(memory_space=pltpu.VMEM)
    dma = pltpu.SemaphoreType.DMA
    bf16 = jnp.bfloat16
    return pl.pallas_call(
        contract,
        out_shape=jax.ShapeDtypeStruct((RING * block, nvir), bf16),
        in_specs=[pl.BlockSpec(memory_space=pltpu.SMEM), vmem, vmem, vmem, pl.BlockSpec(memory_space=pl.ANY)],
        out_specs=vmem,
        scratch_shapes=[
            pltpu.VMEM((ab // rows, rows, cd_here), bf16),
            pltpu.VMEM((pairs, cd), bf16),
            pltpu.VMEM((cd // nvir * pairs, nvir), bf16),
            pltpu.VMEM((CLASSES, cd // nvir * pairs, LANES), jnp.float32),
            pltpu.VMEM((2, CLASSES, pairs, depth), bf16),
            pltpu.VMEM((nvir, LANES), bf16),
            pltpu.VMEM((ab, width), bf16),
            pltpu.VMEM((PER_OWNER, tall, width), bf16),
            pltpu.VMEM((2, CLASSES // 2 * SLOTS, nvir), bf16),
            pltpu.VMEM((RING, PER_OWNER, block, depth), bf16),
            pltpu.VMEM((PER_OWNER, tall, depth), bf16),
            pltpu.VMEM((RING, PER_OWNER, tall, block), bf16),
            pltpu.VMEM((2, RING, CLASSES // 2 * SLOTS, block), bf16),
            dma((ab // rows,)),
            *[dma((PER_OWNER, 8))] * 2,
            *[dma((1,))] * 2,
            *[dma((PER_OWNER, 4))] * 2,
            *[dma((PER_OWNER, 3))] * 2,
            *[dma((PER_OWNER, 6))] * 2,
            *[dma((PER_OWNER, 16))] * 2,
        ],
        compiler_params=pltpu.CompilerParams(
            collective_id=0, has_side_effects=True, vmem_limit_bytes=38 * MIB
        ),
        name="contract",
    )(code, code[:, None], code[None, :], amplitudes, integrals)


def local(amplitudes, integrals, orbital_irrep, orbital_spin):
    group = orbital_irrep + 8 * orbital_spin
    count = jnp.arange(group.shape[0], dtype=jnp.int32)
    earlier = (group[:, None] == group[None, :]) & (count[None, :] < count[:, None])
    rank = jnp.sum(earlier.astype(jnp.int32), axis=1)
    return lax.cond(
        jnp.max(rank) < SLOTS,
        blocked,
        lambda code, *args: dense(*args),
        group * LANES + rank,
        amplitudes,
        integrals,
        orbital_irrep,
        orbital_spin,
    )


def solution(mesh):
    placed = (P(("row", "col"), None), P("col", "row"), P(), P())
    return jax.shard_map(
        local, mesh=mesh, in_specs=placed, out_specs=P("row", "col"), check_vma=False
    )
```
